32 devices in a mesh: ens: 2 (over y), lat: 4 (over x, core), lon: 4 (over z).
Axes of the slice: x: 2, y: 2, z: 4, core: 2. Of those that a mesh axis runs over, the one named last changes fastest.
Arguments:
- tokens: bfloat16 [176, 44, 1024], P(('ens', 'lat'), 'lon'), parts along dimension 0, may hold values from -6 to 6
- qkv_weight: bfloat16 [2, 1024, 1280], P(None, None, 'lon'), may hold values from -4 to 4
- out_weight: bfloat16 [2, 1024, 1024], P(None, None, 'lon'), may hold values from -0.1875 to 0.1875
- norm_gain: float32 [2, 1024], replicated, may hold values from 0.5 to 1.5
- conv_weight: bfloat16 [9, 1024], replicated, may hold values from -4 to 4
- conv_bias: bfloat16 [1024], replicated, may hold values from -6 to 6
Outputs:
- result: bfloat16 [176, 44, 1024], P(('ens', 'lat'), 'lon'), parts along dimension 0
The draws below stay inside these ranges and needn't reach their ends.
There are 2 independent parts, one for each index of `ens`. The reference program is written for one: setup_inputs(seed, part) draws one part's arguments, and reference() takes and returns one part's arrays. A program takes and returns all parts, laid end to end along the dimension named above; an argument that names none is the same for every part. Nothing has to cross between parts.
All inputs are finite; a program needn't handle non-finite values.
Results may differ from the reference program's by a relative error of at most 0.04.
Values may be sent and summed in bfloat16 or wider, within the bound.
A program may use at most 64 MiB of HBM per device.

```python
import jax
import jax.numpy as jnp
from jax import lax

D = 1024
HEADS = 16
KV = 2
HD = 64
QKV = 1280
LATS = 88
LONS = 44


def draw_qkv_weight(key, part):
    normal_base = jnp.clip(jax.random.normal(key, (2, D, QKV), jnp.float32), -6.0, 6.0) * D ** (-0.5)
    return normal_base.astype(jnp.bfloat16)


def block_levels(key, dims, shards, smallest, top_value):
    loudness = 1.0
    for dim, parts in shards:
        heights = jax.random.uniform(jax.random.fold_in(jax.random.fold_in(key, 6), dim), (parts,), jnp.float32, smallest / len(shards), top_value / len(shards))
        loudness = loudness * jnp.repeat(jnp.exp(heights), dims[dim] // parts).reshape((-1,) + (1,) * (len(dims) - 1 - dim))
    return loudness


def bell_draw(stream_key, shape, width, most, cuts=(), kind=jnp.bfloat16):
    array = jax.random.normal(stream_key, shape, jnp.float32) * width
    if len(cuts) > 0:
        array = block_levels(stream_key, shape, cuts, -0.22, 0.18) * array
    return jnp.clip(array, min=-most, max=most).astype(kind)


def setup_inputs(seed: int = 0, part: int = 0) -> dict:
    key_of = jax.random.split(jax.random.key(seed), 7)
    own_keys = jax.random.split(jax.random.fold_in(key_of[6], part), 7)
    tokens = bell_draw(own_keys[0], (LATS, LONS, D), 1.0, 6.0, ((0, 4), (1, 4)))
    qkv_weight = draw_qkv_weight(jax.random.fold_in(key_of[6], 71), part)
    out_weight = bell_draw(key_of[2], (2, D, D), D ** -0.5, 0.1875, ((2, 4),))
    norm_gain = jnp.clip(1.0 + 0.1 * jax.random.normal(key_of[3], (2, D), jnp.float32), 0.5, 1.5)
    conv_weight = bell_draw(key_of[4], (9, D), 0.3, 4.0)
    conv_bias = bell_draw(key_of[5], (D,), 0.5, 6.0)
    return {"tokens": tokens, "qkv_weight": qkv_weight, "out_weight": out_weight, "norm_gain": norm_gain, "conv_weight": conv_weight, "conv_bias": conv_bias}


def split_keyval(keyval):
    batch, length, columns = keyval.shape
    keys = keyval[..., :KV * HD].reshape(batch, length, KV, HD)
    values = keyval[..., KV * HD:].reshape(batch, length, KV, HD)
    return (keys, values)

def attend_lines(query, keyval):
    batch, length, feature = query.shape
    keys, values = split_keyval(keyval)
    grouped = query.reshape(batch, length, KV, HEADS // KV, HD)
    scores = jnp.einsum('nqgjd,nkgd->ngjqk', grouped.astype(jnp.float32), keys.astype(jnp.float32)) * HD ** (-0.5)
    peak = lax.optimization_barrier(jnp.max(scores, axis=-1, keepdims=True))
    expon = jnp.exp(scores - peak)
    denominator = lax.optimization_barrier(jnp.sum(expon, axis=-1))
    weights = expon.astype(jnp.bfloat16)
    mixed = jnp.einsum('ngjqk,nkgd->nqgjd', weights.astype(jnp.float32), values.astype(jnp.float32))
    mixed = mixed / jnp.transpose(denominator, (0, 3, 1, 2))[..., None]
    return mixed.reshape(batch, length, feature).astype(jnp.bfloat16)

def attend_single(line_pair):
    query, keyval = line_pair
    return attend_lines(query[None], keyval[None])[0]

def rms_norm(current, gain):
    values = current.astype(jnp.float32)
    scaled = values * lax.rsqrt(lax.optimization_barrier(jnp.mean(values * values, axis=-1, keepdims=True)) + 1e-06)
    return (scaled * gain.astype(jnp.float32)).astype(jnp.bfloat16)

def reference(tokens, qkv_weight, out_weight, norm_gain, conv_weight, conv_bias):
    lat_rows, lon_cols, feature = tokens.shape
    values = tokens.astype(jnp.float32)
    padded = jnp.pad(values, ((1, 1), (0, 0), (0, 0)))
    padded = jnp.concatenate([padded[:, -1:], padded, padded[:, :1]], axis=1)
    total = values + conv_bias.astype(jnp.float32)
    for shift_lat in range(3):
        for shift_lon in range(3):
            total = total + conv_weight[3 * shift_lat + shift_lon].astype(jnp.float32) * padded[shift_lat:shift_lat + lat_rows, shift_lon:shift_lon + lon_cols]
    current = total.astype(jnp.bfloat16)
    for section_index in range(2):
        normed = rms_norm(current, norm_gain[section_index])
        projected = jnp.dot(normed.reshape(-1, feature), qkv_weight[section_index], preferred_element_type=jnp.float32)
        projected = projected.astype(jnp.bfloat16).reshape(lat_rows, lon_cols, -1)
        if section_index == 0:
            attended = lax.map(attend_single, (projected[..., :feature], projected[..., feature:]))
        else:
            turned = jnp.transpose(projected, (1, 0, 2))
            attended = lax.map(attend_single, (turned[..., :feature], turned[..., feature:]))
            attended = jnp.transpose(attended, (1, 0, 2))
        output = jnp.dot(attended.reshape(-1, feature), out_weight[section_index], preferred_element_type=jnp.float32)
        current = (current.astype(jnp.float32) + output.reshape(lat_rows, lon_cols, feature)).astype(jnp.bfloat16)
    return current
```

```python
import functools

import jax
import jax.numpy as jnp
from jax import lax
from jax.experimental import pallas as pl
from jax.experimental.pallas import tpu as pltpu
from jax.sharding import PartitionSpec as P

HEADS = 16
KV = 2
HD = 64


def with_halo(cells, sides, width, closed):
    for axis, dim in sides:
        count = lax.axis_size(axis)
        ends = count if closed else count - 1
        head = lax.slice_in_dim(cells, 0, width, axis=dim)
        tail = lax.slice_in_dim(cells, cells.shape[dim] - width, cells.shape[dim], axis=dim)
        cells = jnp.concatenate(
            [
                lax.ppermute(tail, axis, [(i, (i + 1) % count) for i in range(ends)]),
                cells,
                lax.ppermute(head, axis, [((i + 1) % count, i) for i in range(ends)]),
            ],
            axis=dim,
        )
    return cells


def split_keyval(keyval):
    batch, length, columns = keyval.shape
    keys = keyval[..., : KV * HD].reshape(batch, length, KV, HD)
    values = keyval[..., KV * HD :].reshape(batch, length, KV, HD)
    return (keys, values)


def line_scores(query, keys):
    batch, length, feature = query.shape
    grouped = query.reshape(batch, length, KV, HEADS // KV, HD)
    return jnp.einsum(
        "nqgjd,nkgd->ngjqk", grouped, keys, preferred_element_type=jnp.float32
    ) * HD ** (-0.5)


def attend_lines(query, keyval):
    batch, length, feature = query.shape
    keys, values = split_keyval(keyval)
    scores = line_scores(query, keys)
    peak = jnp.max(scores, axis=-1, keepdims=True)
    expon = jnp.exp(scores - peak)
    denominator = jnp.sum(expon, axis=-1)
    mixed = jnp.einsum(
        "ngjqk,nkgd->nqgjd", expon.astype(jnp.bfloat16), values, preferred_element_type=jnp.float32
    )
    mixed = mixed / jnp.transpose(denominator, (0, 3, 1, 2))[..., None]
    return mixed.reshape(batch, length, feature).astype(jnp.bfloat16)


def rms_norm(current, gain):
    values = current.astype(jnp.float32)
    scaled = values * lax.rsqrt(jnp.mean(values * values, axis=-1, keepdims=True) + 1e-06)
    return (scaled * gain).astype(jnp.bfloat16)


def shards(tokens, qkv_weight, out_weight, norm_gain, conv_weight, conv_bias):
    lat_rows, lon_cols, feature = tokens.shape
    widened = with_halo(tokens, (("lon", 1),), 1, True)
    padded = with_halo(widened, (("lat", 0),), 1, False)
    total = tokens.astype(jnp.float32) + conv_bias.astype(jnp.float32)
    for shift_lat in range(3):
        for shift_lon in range(3):
            window = padded[
                shift_lat : shift_lat + lat_rows, shift_lon : shift_lon + lon_cols
            ].astype(jnp.float32)
            total = total + conv_weight[3 * shift_lat + shift_lon].astype(jnp.float32) * window
    current = total.astype(jnp.bfloat16)
    for section_index in range(2):
        weight_in, weight_out = (
            lax.all_gather(qkv_weight[section_index], "lon", axis=1, tiled=True),
            lax.all_gather(out_weight[section_index], "lon", axis=1, tiled=True),
        )
        normed = rms_norm(current, norm_gain[section_index])
        projected = jnp.dot(
            normed.reshape(-1, feature), weight_in, preferred_element_type=jnp.float32
        )
        projected = projected.astype(jnp.bfloat16).reshape(lat_rows, lon_cols, -1)
        query = projected[..., :feature]
        keyval = projected[..., feature:]
        if section_index == 0:
            gathered = lax.all_gather(keyval, "lon", axis=1, tiled=True)
            attended = attend_lines(query, gathered)
        else:
            gathered = lax.all_gather(keyval, "lat", axis=0, tiled=True)
            attended = attend_lines(
                jnp.transpose(query, (1, 0, 2)), jnp.transpose(gathered, (1, 0, 2))
            )
            attended = jnp.transpose(attended, (1, 0, 2))
        output = jnp.dot(
            attended.reshape(-1, feature), weight_out, preferred_element_type=jnp.float32
        )
        current = (
            current.astype(jnp.float32) + output.reshape(lat_rows, lon_cols, feature)
        ).astype(jnp.bfloat16)
    return current


MESH = pl.DeviceIdType.MESH
F32 = jnp.float32
BF16 = jnp.bfloat16
STEP0, STEP1, PACKED = 16, 32, 256


def remote(src, dst, send, recv, device):
    return pltpu.make_async_remote_copy(
        src_ref=src, dst_ref=dst, send_sem=send, recv_sem=recv, device_id=device, device_id_type=MESH
    )


def step_kernel(
    tokens_in, wq_in, wo_in, gain, conv_w, conv_b, out,
    tokens, wq, wo, pad, edgef, edge, corner, hcol, hrow, hcor, cur, normed, turned, turn, squeeze, expand,
    proj, att, kvs0, kv0, kvt, kvs1, kv1, kvl,
    sem_t, sem_l, sem_zs, sem_w, sem_fs, sem_c, sem_cs, sem_hs, sem_hr, sem_ks, sem_kr, sem_js, sem_jr,
):
    cols, rows, feature = tokens.shape
    nlon, nlat = 4, 4
    count = rows * STEP0
    ens, lat, lon = lax.axis_index("ens"), lax.axis_index("lat"), lax.axis_index("lon")
    xpos, core = lat // 2, lax.rem(lat, 2)

    wide = wq_in.shape[1]
    width = wo_in.shape[2]
    dev_core = (ens, 2 * xpos + 1 - core, lon)
    dev_x = (ens, 2 * (1 - xpos) + core, lon)
    dev_y = (1 - ens, lat, lon)
    here, at_x, at_y, at_xy = 2 * ens + xpos, 2 * ens + 1 - xpos, 2 * (1 - ens) + xpos, 2 * (1 - ens) + 1 - xpos
    others = (1 + lax.rem(lon, 2), lax.rem(2 + 3 * lon, 5), 3 * (1 - lon // 2))
    inner = (lon == 1) | (lon == 2)
    west, east = lax.rem(lon + 3, 4), lax.rem(lon + 1, 4)
    north, south = lax.rem(lat + 3, 4), lax.rem(lat + 1, 4)
    lat_core, lat_x, lat_xc = 2 * xpos + 1 - core, 2 * (1 - xpos) + core, 2 * (1 - xpos) + 1 - core

    barrier = pltpu.get_barrier_semaphore()
    greet = [(ens, lat, lax.rem(lon + d, 4)) for d in (1, 2, 3)]
    greet += [(ens, lax.rem(lat + d, 4), lon) for d in (1, 2, 3)]
    greet += [(ens, a, b) for a in (north, south) for b in (west, east)]
    greet += [dev_y]
    for device in greet:
        pl.semaphore_signal(barrier, inc=1, device_id=device, device_id_type=MESH)

    def piece(m, chip):
        if m % 2:
            part = width * 4 // 8
            return pl.ds(pl.multiple_of(core * (feature // 2) + chip * part, part), part), pl.ds(0, width)
        part = wide // 4
        half = feature // 2
        return pl.ds(pl.multiple_of(chip * part, 16), part), pl.ds(pl.multiple_of(core * half, half), half)

    def full(m):
        return (wo if m % 2 else wq).at[m // 2]

    def half_of(m, s, which):
        half = feature // 2
        spot = pl.ds(pl.multiple_of(which * half, half), half)
        return full(m).at[s, spot, :] if m % 2 else full(m).at[s, :, spot]

    def own(m):
        return (wo_in if m % 2 else wq_in).at[m // 2]

    load = pltpu.make_async_copy(tokens_in, tokens, sem_t)
    load.start()
    locals_ = [pltpu.make_async_copy(own(m), full(m).at[lon], sem_l.at[m]) for m in range(4)]

    cur[...] = jnp.zeros_like(cur)
    normed[...] = jnp.zeros_like(normed)

    def select(shape, index_of):
        to = lax.broadcasted_iota(jnp.int32, (shape[0], 1), 0)
        fro = lax.broadcasted_iota(jnp.int32, shape, 1)
        return jnp.where(fro == index_of(to), 1.0, 0.0).astype(BF16)

    turn[0] = select((count, count), lambda t: jnp.where(
        lax.rem(t, STEP0) < cols, lax.rem(t, STEP0) * STEP1 + t // STEP0, -1))
    turn[1] = select((count, count), lambda t: jnp.where(
        lax.rem(t, STEP1) < rows, lax.rem(t, STEP1) * STEP0 + t // STEP1, -1))
    squeeze[...] = select((PACKED, count), lambda t: jnp.where(
        t < cols * rows, (t // rows) * STEP1 + lax.rem(t, rows), -1))
    expand[0] = select((count, PACKED), lambda t: jnp.where(
        lax.rem(t, STEP0) < cols, lax.rem(t, STEP0) * rows + t // STEP0, -1))
    expand[1] = select((count, PACKED), lambda t: jnp.where(
        lax.rem(t, STEP1) < rows, (t // STEP1) * rows + lax.rem(t, STEP1), -1))

    load.wait()
    edgef[...] = jnp.zeros_like(edgef)
    for j in range(cols):
        line = tokens[j].astype(F32)
        pad[1 + j, 8 : 8 + rows, :] = line
        edgef[0, j : j + 1, :] = line[0:1]
        edgef[1, j : j + 1, :] = line[rows - 1 : rows]
        if j in (0, cols - 1):
            for a, r in ((0, 0), (1, rows - 1)):
                for b in range(8):
                    corner[a, j // (cols - 1), b : b + 1, :] = line[r : r + 1, 128 * b : 128 * b + 128]
    edge[...] = edgef[...].astype(BF16)

    pl.semaphore_wait(barrier, len(greet))

    pending = []

    def launch(copy):
        copy.start()
        pending.append(copy)

    def send_z(m, which=(0, 1, 2)):
        at, lanes = piece(m, here)

        def copy(k):
            return remote(
                own(m).at[at, lanes], full(m).at[lon, at, lanes],
                sem_zs.at[m, k], sem_w.at[m, lon, here], (ens, lat, others[k]),
            )

        for k in which:
            if k < 2:
                launch(copy(k))
            else:
                @pl.when(inner)
                def _():
                    copy(2).start()

    def arrived(m, s, chip):
        at, lanes = piece(m, chip)
        spot = full(m).at[s, at, lanes]
        remote(spot, spot, sem_zs.at[m, 0], sem_w.at[m, s, chip], dev_core).wait_recv()

    def pass_on(m, s, chip, send, device):
        at, lanes = piece(m, chip)
        spot = full(m).at[s, at, lanes]
        return remote(spot, spot, send, sem_w.at[m, s, chip], device)

    def z_in(m, i):
        s = others[i]
        arrived(m, s, here)
        launch(pass_on(m, s, here, sem_fs.at[m, i, 0], dev_x))
        launch(pass_on(m, s, here, sem_fs.at[m, i, 1], dev_y))
        if i == 2:
            @pl.when(inner)
            def _():
                pass_on(m, s, here, sem_zs.at[m, 3], (ens, lat, others[1])).start()

    def xy_in(m, i):
        s = others[i]
        arrived(m, s, at_x)
        if (m + i) % 2 == 0:
            launch(pass_on(m, s, at_x, sem_fs.at[m, i, 2], dev_y))
        arrived(m, s, at_y)
        if (m + i) % 2 == 1:
            launch(pass_on(m, s, at_y, sem_fs.at[m, i, 2], dev_x))

    def diag_in(m, i):
        s = others[i]
        arrived(m, s, at_xy)
        launch(remote(half_of(m, s, core), half_of(m, s, core), sem_cs.at[m, i], sem_c.at[m, i], dev_core))

    def whole(m, i):
        spot = half_of(m, others[i], 1 - core)
        remote(spot, spot, sem_cs.at[m, i], sem_c.at[m, i], dev_core).wait_recv()

    halos = [
        (tokens.at[cols - 1], hcol.at[0], (ens, lat, east)),
        (tokens.at[0], hcol.at[1], (ens, lat, west)),
        (edge.at[1], hrow.at[0], (ens, south, lon)),
        (edge.at[0], hrow.at[1], (ens, north, lon)),
        (corner.at[1, 1], hcor.at[0], (ens, south, east)),
        (corner.at[1, 0], hcor.at[1], (ens, south, west)),
        (corner.at[0, 1], hcor.at[2], (ens, north, east)),
        (corner.at[0, 0], hcor.at[3], (ens, north, west)),
    ]
    hcopies = [remote(a, b, sem_hs.at[k], sem_hr.at[k], dev) for k, (a, b, dev) in enumerate(halos)]

    def halo_in():
        for copy in hcopies:
            copy.wait_recv()
        for side, place in ((0, 0), (1, 1 + cols)):
            pad[place, 8 : 8 + rows, :] = hcol[side].astype(F32)
        for k, (spot, inside) in enumerate(((7, lat > 0), (8 + rows, lat < nlat - 1))):
            keep = jnp.where(inside, 1.0, 0.0).astype(F32)
            line = hrow[k].astype(F32) * keep
            for j in range(cols):
                pad[1 + j, spot : spot + 1, :] = line[j : j + 1]
            for b in range(8):
                lanes = slice(128 * b, 128 * b + 128)
                pad[0, spot : spot + 1, lanes] = hcor[2 * k, b : b + 1, :] * keep
                pad[1 + cols, spot : spot + 1, lanes] = hcor[2 * k + 1, b : b + 1, :] * keep

    sent = 24

    def rms(values, k):
        scaled = values * lax.rsqrt(jnp.mean(values * values, axis=-1, keepdims=True) + 1e-06)
        return (scaled * gain[k : k + 1, :]).astype(BF16)

    def conv(low, high):
        taps = conv_w[...].astype(F32)
        bias = conv_b[...].astype(F32).reshape(1, feature)
        alive = lax.broadcasted_iota(jnp.int32, (sent, 1), 0) < rows

        def conv_line(j, carry):
            total = pad[j + 1, 8 : 8 + sent, :] + bias
            for a in range(3):
                for b in range(3):
                    total = total + taps[3 * a + b : 3 * a + b + 1] * pad[j + b, 7 + a : 7 + a + sent, :]
            total = jnp.where(alive, total, 0.0)
            rounded = jnp.concatenate([total, jnp.zeros((STEP1 - sent, feature), F32)], axis=0).astype(BF16)
            spot = pl.ds(pl.multiple_of(j * STEP1, STEP1), STEP1)
            cur[spot, :] = rounded
            normed[spot, :] = rms(rounded.astype(F32), 0)
            return carry

        lax.fori_loop(low, high, conv_line, 0, unroll=True)

    def halves(block):
        left = lax.broadcasted_iota(jnp.int32, block.shape, 1) < HD
        swapped = jnp.concatenate([block[:, HD:], block[:, :HD]], axis=1)
        zero = jnp.zeros_like(block)
        keys = (jnp.where(left, block, zero), jnp.where(left, zero, swapped))
        values = (jnp.where(left, swapped, zero), jnp.where(left, zero, block))
        return keys, values

    def contract(a, b):
        return lax.dot_general(a, b, (((1,), (1,)), ((), ())), preferred_element_type=F32)

    def attend(g, block_of, span, low, high, step, valid):
        pairs = HEADS // KV // 2

        def body(r, carry):
            spot = pl.ds(pl.multiple_of(r * step, step), step)
            kh, vh = halves(block_of(spot))
            sides = lax.broadcasted_iota(jnp.int32, (span, 2 * HD), 1) < HD
            ones = [jnp.where(sides, 1.0, 0.0).astype(BF16), jnp.where(sides, 0.0, 1.0).astype(BF16)]
            lane = lax.broadcasted_iota(jnp.int32, (1, span), 1)
            valid_key = lax.rem(lane, step) < valid
            base = g * pairs
            query = jnp.concatenate(
                [proj[spot, (base + p) * 128 : (base + p + 1) * 128] for p in range(pairs)], axis=0
            )
            blend = [jnp.concatenate([vh[half], ones[half]], axis=1) for half in range(2)]
            both = None
            for half in range(2):
                scores = jnp.where(valid_key, contract(query, kh[half]), -jnp.inf)
                expon = jnp.exp(scores - jnp.max(scores, axis=-1, keepdims=True))
                term = jnp.dot(expon.astype(BF16), blend[half], preferred_element_type=F32)
                both = term if both is None else both + term
            mixed = (both[:, : 2 * HD] / both[:, 2 * HD :]).astype(BF16)
            for p in range(pairs):
                att[spot, (base + p) * 128 : (base + p + 1) * 128] = mixed[p * step : (p + 1) * step]
            return carry

        lax.fori_loop(low, high, body, 0, unroll=True)

    def wide_rows(k, low, high):
        return wq.at[k].reshape(nlon * wide, feature)[low:high, :]

    def query_of(k, source, low, high):
        for t in range(low, high, 256):
            proj[:, t : t + 256] = (contract(source[...], wide_rows(k, t, t + 256)) * HD ** (-0.5)).astype(BF16)

    def keyval_rows(k, g):
        low = feature + g * HD
        return [wide_rows(k, low, low + HD), wide_rows(k, low + KV * HD, low + KV * HD + HD)]

    def send_kv0(g):
        kvs0[g] = jnp.dot(
            squeeze[...], contract(normed[...], jnp.concatenate(keyval_rows(0, g), axis=0)).astype(BF16),
            preferred_element_type=F32,
        ).astype(BF16)

        def copy(k):
            return remote(
                kvs0.at[g], kv0.at[g, lon], sem_ks.at[g, k], sem_kr.at[g, lon], (ens, lat, others[k])
            )

        launch(copy(0))
        launch(copy(1))

        @pl.when(inner)
        def _():
            copy(2).start()

        kv0[g, lon] = kvs0[g]

    def kv0_in(g, i):
        spot = kv0.at[g, others[i]]
        remote(spot, spot, sem_ks.at[g, 0], sem_kr.at[g, others[i]], dev_core).wait_recv()

    def relay_kv0(g):
        kv0_in(g, 2)

        @pl.when(inner)
        def _():
            spot = kv0.at[g, others[2]]
            remote(spot, spot, sem_ks.at[g, 3], sem_kr.at[g, others[2]], (ens, lat, others[1])).start()

    def unfold0(g):
        for s in range(nlon):
            kvt[g, s] = jnp.dot(expand[0], kv0[g, s], preferred_element_type=F32).astype(BF16)

    def send_kv1():
        mixed = contract(normed[...], jnp.concatenate(keyval_rows(1, 0) + keyval_rows(1, 1), axis=0)).astype(BF16)
        kvs1[...] = jnp.dot(squeeze[...], mixed, preferred_element_type=F32).astype(BF16)
        launch(remote(kvs1, kv1.at[lat], sem_js.at[0], sem_jr.at[lat], dev_x))
        launch(remote(kvs1, kv1.at[lat], sem_js.at[1], sem_jr.at[lat], dev_core))
        kvl[lat] = mixed

    def kv1_in(s):
        spot = kv1.at[s]
        remote(spot, spot, sem_js.at[0], sem_jr.at[s], dev_core).wait_recv()

    def share_kv1():
        kv1_in(lat_x)
        launch(remote(kv1.at[lat_x], kv1.at[lat_x], sem_js.at[2], sem_jr.at[lat_x], dev_core))

    def unfold1(s):
        kvl[s] = jnp.dot(expand[1], kv1[s], preferred_element_type=F32).astype(BF16)

    def back(k, values, s):
        lanes = pl.ds(pl.multiple_of(s * width, width), width)
        return (cur[:, lanes].astype(F32) + jnp.dot(values[...], wo[k, s], preferred_element_type=F32)).astype(BF16)

    def gathered(g):
        return lambda spot: jnp.concatenate([kvt[g, s, spot, :] for s in range(nlon)], axis=0)

    def lined(g):
        return lambda spot: jnp.concatenate(
            [kvl[s, spot, g * 128 : g * 128 + 128] for s in range(nlat)], axis=0
        )

    def norm_row(i, carry):
        spot = pl.ds(pl.multiple_of(i * STEP1, STEP1), STEP1)
        normed[spot, :] = rms(cur[spot, :].astype(F32), 1)
        return carry

    def back0():
        for s in range(nlon):
            cur[:, s * width : (s + 1) * width] = back(0, turned, s)

    def back1(s):
        lanes = pl.ds(pl.multiple_of(s * width, width), width)
        out[:, :, lanes] = back(1, att, s).reshape(cols, STEP1, width)[:, :rows, :]

    def attend0(g, low, high):
        attend(g, gathered(g), nlon * STEP0, low, high, STEP0, cols)

    def attend1(g, low, high):
        attend(g, lined(g), nlat * STEP1, low, high, STEP1, rows)

    for copy in locals_:
        copy.start()
    send_z(0, (0, 1, 2))
    for copy in hcopies:
        copy.start()
    z_in(0, 0)
    send_z(1, (0, 1, 2))
    z_in(0, 1)
    z_in(0, 2)
    halo_in()
    xy_in(0, 0)
    xy_in(0, 1)
    z_in(1, 0)
    xy_in(0, 2)
    conv(0, 6)
    z_in(1, 1)
    z_in(1, 2)
    conv(6, cols)
    diag_in(0, 0)
    diag_in(0, 1)
    diag_in(0, 2)
    turned[...] = jnp.dot(turn[0], normed[...], preferred_element_type=F32).astype(BF16)
    whole(0, 0)
    whole(0, 1)
    whole(0, 2)
    locals_[0].wait()
    send_kv0(0)
    send_kv0(1)
    query_of(0, turned, 0, feature // 2)
    send_z(2, (0, 1, 2))
    query_of(0, turned, feature // 2, feature)
    xy_in(1, 0)
    relay_kv0(0)
    xy_in(1, 1)
    xy_in(1, 2)
    kv0_in(0, 0)
    kv0_in(0, 1)
    z_in(2, 0)
    unfold0(0)
    z_in(2, 1)
    z_in(2, 2)
    attend0(0, 0, rows // 2)
    attend0(0, rows // 2, rows)
    relay_kv0(1)
    diag_in(1, 0)
    diag_in(1, 1)
    diag_in(1, 2)
    kv0_in(1, 0)
    kv0_in(1, 1)
    xy_in(2, 0)
    xy_in(2, 1)
    unfold0(1)
    xy_in(2, 2)
    attend0(1, 0, rows // 2)
    send_z(3, (0, 1, 2))
    attend0(1, rows // 2, rows)
    turned[...] = jnp.dot(turn[1], att[...], preferred_element_type=F32).astype(BF16)
    diag_in(2, 0)
    diag_in(2, 1)
    diag_in(2, 2)
    whole(1, 0)
    whole(1, 1)
    whole(1, 2)
    z_in(3, 0)
    locals_[1].wait()
    back0()
    z_in(3, 1)
    z_in(3, 2)
    lax.fori_loop(0, count // STEP1, norm_row, 0, unroll=True)
    whole(2, 0)
    whole(2, 1)
    whole(2, 2)
    locals_[2].wait()
    send_kv1()
    query_of(1, normed, 0, feature // 2)
    query_of(1, normed, feature // 2, feature)
    share_kv1()
    xy_in(3, 0)
    unfold1(lat_x)
    kv1_in(lat_core)
    unfold1(lat_core)
    xy_in(3, 1)
    kv1_in(lat_xc)
    xy_in(3, 2)
    unfold1(lat_xc)
    attend1(0, 0, 6)
    diag_in(3, 0)
    attend1(0, 6, cols)
    attend1(1, 0, 6)
    diag_in(3, 1)
    attend1(1, 6, cols)
    diag_in(3, 2)
    locals_[3].wait()
    back1(lon)
    whole(3, 0)
    back1(others[0])
    whole(3, 1)
    back1(others[1])
    whole(3, 2)
    back1(others[2])
    for copy in hcopies + pending:
        copy.wait_send()

    @pl.when(inner)
    def _():
        for m in range(4):
            at, lanes = piece(m, here)
            spot = full(m).at[0, at, lanes]
            for k in (2, 3):
                remote(spot, spot, sem_zs.at[m, k], sem_w.at[m, 0, here], dev_core).wait_send()
        for g in range(KV):
            for k in (2, 3):
                remote(kvs0.at[g], kvs0.at[g], sem_ks.at[g, k], sem_kr.at[g, 0], dev_core).wait_send()


def fused(tokens, qkv_weight, out_weight, norm_gain, conv_weight, conv_bias, nlat, nlon):
    tokens, qkv_weight = jnp.swapaxes(tokens, 0, 1), jnp.swapaxes(qkv_weight, 1, 2)
    cols, rows, feature = tokens.shape
    count = rows * STEP0
    vmem = pl.BlockSpec(memory_space=pltpu.VMEM)
    hbm = pl.BlockSpec(memory_space=pl.ANY)
    dma = pltpu.SemaphoreType.DMA
    result = pl.pallas_call(
        step_kernel,
        out_shape=jax.ShapeDtypeStruct(tokens.shape, BF16),
        in_specs=[hbm, hbm, hbm, vmem, vmem, vmem],
        out_specs=vmem,
        scratch_shapes=[
            pltpu.VMEM(tokens.shape, BF16),
            pltpu.VMEM((2, nlon) + qkv_weight.shape[1:], BF16),
            pltpu.VMEM((2, nlon) + out_weight.shape[1:], BF16),
            pltpu.VMEM((cols + 2, 40, feature), F32),
            pltpu.VMEM((2, 16, feature), F32),
            pltpu.VMEM((2, 16, feature), BF16),
            pltpu.VMEM((2, 2, 8, 128), F32),
            pltpu.VMEM((2, rows, feature), BF16),
            pltpu.VMEM((2, 16, feature), BF16),
            pltpu.VMEM((4, 8, 128), F32),
            pltpu.VMEM((count, feature), BF16),
            pltpu.VMEM((count, feature), BF16),
            pltpu.VMEM((count, feature), BF16),
            pltpu.VMEM((2, count, count), BF16),
            pltpu.VMEM((PACKED, count), BF16),
            pltpu.VMEM((2, count, PACKED), BF16),
            pltpu.VMEM((count, feature), BF16),
            pltpu.VMEM((count, feature), BF16),
            pltpu.VMEM((KV, PACKED, 2 * HD), BF16),
            pltpu.VMEM((KV, nlon, PACKED, 2 * HD), BF16),
            pltpu.VMEM((KV, nlon, count, 2 * HD), BF16),
            pltpu.VMEM((PACKED, KV * 2 * HD), BF16),
            pltpu.VMEM((nlat, PACKED, KV * 2 * HD), BF16),
            pltpu.VMEM((nlat, count, KV * 2 * HD), BF16),
            dma,
            dma((4,)),
            dma((4, 4)),
            dma((4, nlon, 4)),
            dma((4, 3, 3)),
            dma((4, 3)),
            dma((4, 3)),
            dma((8,)),
            dma((8,)),
            dma((KV, 4)),
            dma((KV, nlon)),
            dma((3,)),
            dma((nlat,)),
        ],
        compiler_params=pltpu.CompilerParams(
            collective_id=0, has_side_effects=True, vmem_limit_bytes=56 * 2**20
        ),
    )(tokens, qkv_weight, out_weight, norm_gain, conv_weight, conv_bias)
    return jnp.swapaxes(result, 0, 1)


def entry(tokens, qkv_weight, out_weight, norm_gain, conv_weight, conv_bias):
    nens, nlat, nlon = (lax.axis_size(name) for name in ("ens", "lat", "lon"))
    if (nens, nlat, nlon) == (2, 4, 4) and tokens.shape[:2] == (22, 11):
        return fused(
            tokens, qkv_weight, out_weight, norm_gain, conv_weight, conv_bias, nlat, nlon
        )
    return shards(tokens, qkv_weight, out_weight, norm_gain, conv_weight, conv_bias)


def solution(mesh):
    in_specs = (
        P(("ens", "lat"), "lon", None),
        P(None, None, "lon"),
        P(None, None, "lon"),
        P(),
        P(),
        P(),
    )
    out_specs = P(("ens", "lat"), "lon", None)
    return jax.shard_map(entry, mesh=mesh, in_specs=in_specs, out_specs=out_specs, check_vma=False)
```

```python
import functools

import jax
import jax.numpy as jnp
from jax import lax
from jax.experimental import pallas as pl
from jax.experimental.pallas import tpu as pltpu
from jax.sharding import PartitionSpec as P

HEADS = 16
KV = 2
HD = 64


def with_halo(cells, sides, width, closed):
    for axis, dim in sides:
        count = lax.axis_size(axis)
        ends = count if closed else count - 1
        head = lax.slice_in_dim(cells, 0, width, axis=dim)
        tail = lax.slice_in_dim(cells, cells.shape[dim] - width, cells.shape[dim], axis=dim)
        cells = jnp.concatenate(
            [
                lax.ppermute(tail, axis, [(i, (i + 1) % count) for i in range(ends)]),
                cells,
                lax.ppermute(head, axis, [((i + 1) % count, i) for i in range(ends)]),
            ],
            axis=dim,
        )
    return cells


def split_keyval(keyval):
    batch, length, columns = keyval.shape
    keys = keyval[..., : KV * HD].reshape(batch, length, KV, HD)
    values = keyval[..., KV * HD :].reshape(batch, length, KV, HD)
    return (keys, values)


def line_scores(query, keys):
    batch, length, feature = query.shape
    grouped = query.reshape(batch, length, KV, HEADS // KV, HD)
    return jnp.einsum(
        "nqgjd,nkgd->ngjqk", grouped, keys, preferred_element_type=jnp.float32
    ) * HD ** (-0.5)


def attend_lines(query, keyval):
    batch, length, feature = query.shape
    keys, values = split_keyval(keyval)
    scores = line_scores(query, keys)
    peak = jnp.max(scores, axis=-1, keepdims=True)
    expon = jnp.exp(scores - peak)
    denominator = jnp.sum(expon, axis=-1)
    mixed = jnp.einsum(
        "ngjqk,nkgd->nqgjd", expon.astype(jnp.bfloat16), values, preferred_element_type=jnp.float32
    )
    mixed = mixed / jnp.transpose(denominator, (0, 3, 1, 2))[..., None]
    return mixed.reshape(batch, length, feature).astype(jnp.bfloat16)


def rms_norm(current, gain):
    values = current.astype(jnp.float32)
    scaled = values * lax.rsqrt(jnp.mean(values * values, axis=-1, keepdims=True) + 1e-06)
    return (scaled * gain).astype(jnp.bfloat16)


def shards(tokens, qkv_weight, out_weight, norm_gain, conv_weight, conv_bias):
    lat_rows, lon_cols, feature = tokens.shape
    widened = with_halo(tokens, (("lon", 1),), 1, True)
    padded = with_halo(widened, (("lat", 0),), 1, False)
    total = tokens.astype(jnp.float32) + conv_bias.astype(jnp.float32)
    for shift_lat in range(3):
        for shift_lon in range(3):
            window = padded[
                shift_lat : shift_lat + lat_rows, shift_lon : shift_lon + lon_cols
            ].astype(jnp.float32)
            total = total + conv_weight[3 * shift_lat + shift_lon].astype(jnp.float32) * window
    current = total.astype(jnp.bfloat16)
    for section_index in range(2):
        weight_in, weight_out = (
            lax.all_gather(qkv_weight[section_index], "lon", axis=1, tiled=True),
            lax.all_gather(out_weight[section_index], "lon", axis=1, tiled=True),
        )
        normed = rms_norm(current, norm_gain[section_index])
        projected = jnp.dot(
            normed.reshape(-1, feature), weight_in, preferred_element_type=jnp.float32
        )
        projected = projected.astype(jnp.bfloat16).reshape(lat_rows, lon_cols, -1)
        query = projected[..., :feature]
        keyval = projected[..., feature:]
        if section_index == 0:
            gathered = lax.all_gather(keyval, "lon", axis=1, tiled=True)
            attended = attend_lines(query, gathered)
        else:
            gathered = lax.all_gather(keyval, "lat", axis=0, tiled=True)
            attended = attend_lines(
                jnp.transpose(query, (1, 0, 2)), jnp.transpose(gathered, (1, 0, 2))
            )
            attended = jnp.transpose(attended, (1, 0, 2))
        output = jnp.dot(
            attended.reshape(-1, feature), weight_out, preferred_element_type=jnp.float32
        )
        current = (
            current.astype(jnp.float32) + output.reshape(lat_rows, lon_cols, feature)
        ).astype(jnp.bfloat16)
    return current


MESH = pl.DeviceIdType.MESH
F32 = jnp.float32
BF16 = jnp.bfloat16
STEP0, STEP1, PACKED = 16, 32, 256


def remote(src, dst, send, recv, device):
    return pltpu.make_async_remote_copy(
        src_ref=src, dst_ref=dst, send_sem=send, recv_sem=recv, device_id=device, device_id_type=MESH
    )


def step_kernel(
    tokens_in, wq_in, wo_in, gain, conv_w, conv_b, out,
    tokens, wq, wo, pad, edgef, edge, corner, hcol, hrow, hcor, cur, normed, turned, turn, squeeze, expand,
    proj, att, kvs0, kv0, kvt, kvs1, kv1, kvl,
    sem_t, sem_l, sem_zs, sem_w, sem_fs, sem_c, sem_cs, sem_hs, sem_hr, sem_ks, sem_kr, sem_js, sem_jr,
):
    cols, rows, feature = tokens.shape
    nlon, nlat = 4, 4
    count = rows * STEP0
    ens, lat, lon = lax.axis_index("ens"), lax.axis_index("lat"), lax.axis_index("lon")
    xpos, core = lat // 2, lax.rem(lat, 2)

    wide = wq_in.shape[1]
    width = wo_in.shape[2]
    dev_core = (ens, 2 * xpos + 1 - core, lon)
    dev_x = (ens, 2 * (1 - xpos) + core, lon)
    dev_y = (1 - ens, lat, lon)
    here, at_x, at_y, at_xy = 2 * ens + xpos, 2 * ens + 1 - xpos, 2 * (1 - ens) + xpos, 2 * (1 - ens) + 1 - xpos
    others = (1 + lax.rem(lon, 2), lax.rem(2 + 3 * lon, 5), 3 * (1 - lon // 2))
    inner = (lon == 1) | (lon == 2)
    west, east = lax.rem(lon + 3, 4), lax.rem(lon + 1, 4)
    north, south = lax.rem(lat + 3, 4), lax.rem(lat + 1, 4)
    lat_core, lat_x, lat_xc = 2 * xpos + 1 - core, 2 * (1 - xpos) + core, 2 * (1 - xpos) + 1 - core

    barrier = pltpu.get_barrier_semaphore()
    greet = [(ens, lat, lax.rem(lon + d, 4)) for d in (1, 2, 3)]
    greet += [(ens, lax.rem(lat + d, 4), lon) for d in (1, 2, 3)]
    greet += [(ens, a, b) for a in (north, south) for b in (west, east)]
    greet += [dev_y]
    for device in greet:
        pl.semaphore_signal(barrier, inc=1, device_id=device, device_id_type=MESH)

    def piece(m, chip):
        if m % 2:
            part = width * 4 // 8
            return pl.ds(pl.multiple_of(core * (feature // 2) + chip * part, part), part), pl.ds(0, width)
        part = wide // 4
        half = feature // 2
        return pl.ds(pl.multiple_of(chip * part, 16), part), pl.ds(pl.multiple_of(core * half, half), half)

    def full(m):
        return (wo if m % 2 else wq).at[m // 2]

    def half_of(m, s, which):
        half = feature // 2
        spot = pl.ds(pl.multiple_of(which * half, half), half)
        return full(m).at[s, spot, :] if m % 2 else full(m).at[s, :, spot]

    def own(m):
        return (wo_in if m % 2 else wq_in).at[m // 2]

    load = pltpu.make_async_copy(tokens_in, tokens, sem_t)
    load.start()
    locals_ = [pltpu.make_async_copy(own(m), full(m).at[lon], sem_l.at[m]) for m in range(4)]

    cur[...] = jnp.zeros_like(cur)
    normed[...] = jnp.zeros_like(normed)

    def select(shape, index_of):
        to = lax.broadcasted_iota(jnp.int32, (shape[0], 1), 0)
        fro = lax.broadcasted_iota(jnp.int32, shape, 1)
        return jnp.where(fro == index_of(to), 1.0, 0.0).astype(BF16)

    turn[0] = select((count, count), lambda t: jnp.where(
        lax.rem(t, STEP0) < cols, lax.rem(t, STEP0) * STEP1 + t // STEP0, -1))
    turn[1] = select((count, count), lambda t: jnp.where(
        lax.rem(t, STEP1) < rows, lax.rem(t, STEP1) * STEP0 + t // STEP1, -1))
    squeeze[...] = select((PACKED, count), lambda t: jnp.where(
        t < cols * rows, (t // rows) * STEP1 + lax.rem(t, rows), -1))
    expand[0] = select((count, PACKED), lambda t: jnp.where(
        lax.rem(t, STEP0) < cols, lax.rem(t, STEP0) * rows + t // STEP0, -1))
    expand[1] = select((count, PACKED), lambda t: jnp.where(
        lax.rem(t, STEP1) < rows, (t // STEP1) * rows + lax.rem(t, STEP1), -1))

    load.wait()
    edgef[...] = jnp.zeros_like(edgef)
    for j in range(cols):
        line = tokens[j].astype(F32)
        pad[1 + j, 8 : 8 + rows, :] = line
        edgef[0, j : j + 1, :] = line[0:1]
        edgef[1, j : j + 1, :] = line[rows - 1 : rows]
        if j in (0, cols - 1):
            for a, r in ((0, 0), (1, rows - 1)):
                for b in range(8):
                    corner[a, j // (cols - 1), b : b + 1, :] = line[r : r + 1, 128 * b : 128 * b + 128]
    edge[...] = edgef[...].astype(BF16)

    pl.semaphore_wait(barrier, len(greet))

    pending = []

    def launch(copy):
        copy.start()
        pending.append(copy)

    def send_z(m, which=(0, 1, 2)):
        at, lanes = piece(m, here)

        def copy(k):
            return remote(
                own(m).at[at, lanes], full(m).at[lon, at, lanes],
                sem_zs.at[m, k], sem_w.at[m, lon, here], (ens, lat, others[k]),
            )

        for k in which:
            if k < 2:
                launch(copy(k))
            else:
                @pl.when(inner)
                def _():
                    copy(2).start()

    def arrived(m, s, chip):
        at, lanes = piece(m, chip)
        spot = full(m).at[s, at, lanes]
        remote(spot, spot, sem_zs.at[m, 0], sem_w.at[m, s, chip], dev_core).wait_recv()

    def pass_on(m, s, chip, send, device):
        at, lanes = piece(m, chip)
        spot = full(m).at[s, at, lanes]
        return remote(spot, spot, send, sem_w.at[m, s, chip], device)

    def z_in(m, i):
        s = others[i]
        arrived(m, s, here)
        launch(pass_on(m, s, here, sem_fs.at[m, i, 0], dev_x))
        launch(pass_on(m, s, here, sem_fs.at[m, i, 1], dev_y))
        if i == 2:
            @pl.when(inner)
            def _():
                pass_on(m, s, here, sem_zs.at[m, 3], (ens, lat, others[1])).start()

    def xy_in(m, i):
        s = others[i]
        arrived(m, s, at_x)
        if (m + i) % 2 == 0:
            launch(pass_on(m, s, at_x, sem_fs.at[m, i, 2], dev_y))
        arrived(m, s, at_y)
        if (m + i) % 2 == 1:
            launch(pass_on(m, s, at_y, sem_fs.at[m, i, 2], dev_x))

    def diag_in(m, i):
        s = others[i]
        arrived(m, s, at_xy)
        launch(remote(half_of(m, s, core), half_of(m, s, core), sem_cs.at[m, i], sem_c.at[m, i], dev_core))

    def whole(m, i):
        spot = half_of(m, others[i], 1 - core)
        remote(spot, spot, sem_cs.at[m, i], sem_c.at[m, i], dev_core).wait_recv()

    halos = [
        (tokens.at[cols - 1], hcol.at[0], (ens, lat, east)),
        (tokens.at[0], hcol.at[1], (ens, lat, west)),
        (edge.at[1], hrow.at[0], (ens, south, lon)),
        (edge.at[0], hrow.at[1], (ens, north, lon)),
        (corner.at[1, 1], hcor.at[0], (ens, south, east)),
        (corner.at[1, 0], hcor.at[1], (ens, south, west)),
        (corner.at[0, 1], hcor.at[2], (ens, north, east)),
        (corner.at[0, 0], hcor.at[3], (ens, north, west)),
    ]
    hcopies = [remote(a, b, sem_hs.at[k], sem_hr.at[k], dev) for k, (a, b, dev) in enumerate(halos)]

    def halo_in():
        for copy in hcopies:
            copy.wait_recv()
        for side, place in ((0, 0), (1, 1 + cols)):
            pad[place, 8 : 8 + rows, :] = hcol[side].astype(F32)
        for k, (spot, inside) in enumerate(((7, lat > 0), (8 + rows, lat < nlat - 1))):
            keep = jnp.where(inside, 1.0, 0.0).astype(F32)
            line = hrow[k].astype(F32) * keep
            for j in range(cols):
                pad[1 + j, spot : spot + 1, :] = line[j : j + 1]
            for b in range(8):
                lanes = slice(128 * b, 128 * b + 128)
                pad[0, spot : spot + 1, lanes] = hcor[2 * k, b : b + 1, :] * keep
                pad[1 + cols, spot : spot + 1, lanes] = hcor[2 * k + 1, b : b + 1, :] * keep

    sent = 24

    def rms(values, k):
        scaled = values * lax.rsqrt(jnp.mean(values * values, axis=-1, keepdims=True) + 1e-06)
        return (scaled * gain[k : k + 1, :]).astype(BF16)

    def conv(low, high):
        taps = conv_w[...].astype(F32)
        bias = conv_b[...].astype(F32).reshape(1, feature)
        alive = lax.broadcasted_iota(jnp.int32, (sent, 1), 0) < rows

        def conv_line(j, carry):
            total = pad[j + 1, 8 : 8 + sent, :] + bias
            for a in range(3):
                for b in range(3):
                    total = total + taps[3 * a + b : 3 * a + b + 1] * pad[j + b, 7 + a : 7 + a + sent, :]
            total = jnp.where(alive, total, 0.0)
            rounded = jnp.concatenate([total, jnp.zeros((STEP1 - sent, feature), F32)], axis=0).astype(BF16)
            spot = pl.ds(pl.multiple_of(j * STEP1, STEP1), STEP1)
            cur[spot, :] = rounded
            normed[spot, :] = rms(rounded.astype(F32), 0)
            return carry

        lax.fori_loop(low, high, conv_line, 0, unroll=True)

    def halves(block):
        left = lax.broadcasted_iota(jnp.int32, block.shape, 1) < HD
        swapped = jnp.concatenate([block[:, HD:], block[:, :HD]], axis=1)
        zero = jnp.zeros_like(block)
        keys = (jnp.where(left, block, zero), jnp.where(left, zero, swapped))
        values = (jnp.where(left, swapped, zero), jnp.where(left, zero, block))
        return keys, values

    def contract(a, b):
        return lax.dot_general(a, b, (((1,), (1,)), ((), ())), preferred_element_type=F32)

    def attend(g, block_of, span, low, high, step, valid):
        pairs = HEADS // KV // 2

        def body(r, carry):
            spot = pl.ds(pl.multiple_of(r * step, step), step)
            kh, vh = halves(block_of(spot))
            sides = lax.broadcasted_iota(jnp.int32, (span, 2 * HD), 1) < HD
            ones = [jnp.where(sides, 1.0, 0.0).astype(BF16), jnp.where(sides, 0.0, 1.0).astype(BF16)]
            lane = lax.broadcasted_iota(jnp.int32, (1, span), 1)
            valid_key = lax.rem(lane, step) < valid
            base = g * pairs
            query = jnp.concatenate(
                [proj[spot, (base + p) * 128 : (base + p + 1) * 128] for p in range(pairs)], axis=0
            )
            blend = [jnp.concatenate([vh[half], ones[half]], axis=1) for half in range(2)]
            both = None
            for half in range(2):
                scores = jnp.where(valid_key, contract(query, kh[half]), -jnp.inf)
                expon = jnp.exp(scores - jnp.max(scores, axis=-1, keepdims=True))
                term = jnp.dot(expon.astype(BF16), blend[half], preferred_element_type=F32)
                both = term if both is None else both + term
            mixed = (both[:, : 2 * HD] / both[:, 2 * HD :]).astype(BF16)
            for p in range(pairs):
                att[spot, (base + p) * 128 : (base + p + 1) * 128] = mixed[p * step : (p + 1) * step]
            return carry

        lax.fori_loop(low, high, body, 0, unroll=True)

    def wide_rows(k, low, high):
        return wq.at[k].reshape(nlon * wide, feature)[low:high, :]

    def query_of(k, source, low, high):
        for t in range(low, high, 256):
            proj[:, t : t + 256] = (contract(source[...], wide_rows(k, t, t + 256)) * HD ** (-0.5)).astype(BF16)

    def keyval_rows(k, g):
        low = feature + g * HD
        return [wide_rows(k, low, low + HD), wide_rows(k, low + KV * HD, low + KV * HD + HD)]

    def send_kv0(g):
        kvs0[g] = jnp.dot(
            squeeze[...], contract(normed[...], jnp.concatenate(keyval_rows(0, g), axis=0)).astype(BF16),
            preferred_element_type=F32,
        ).astype(BF16)

        def copy(k):
            return remote(
                kvs0.at[g], kv0.at[g, lon], sem_ks.at[g, k], sem_kr.at[g, lon], (ens, lat, others[k])
            )

        launch(copy(0))
        launch(copy(1))

        @pl.when(inner)
        def _():
            copy(2).start()

        kv0[g, lon] = kvs0[g]

    def kv0_in(g, i):
        spot = kv0.at[g, others[i]]
        remote(spot, spot, sem_ks.at[g, 0], sem_kr.at[g, others[i]], dev_core).wait_recv()

    def relay_kv0(g):
        kv0_in(g, 2)

        @pl.when(inner)
        def _():
            spot = kv0.at[g, others[2]]
            remote(spot, spot, sem_ks.at[g, 3], sem_kr.at[g, others[2]], (ens, lat, others[1])).start()

    def unfold0(g):
        for s in range(nlon):
            kvt[g, s] = jnp.dot(expand[0], kv0[g, s], preferred_element_type=F32).astype(BF16)

    def send_kv1():
        mixed = contract(normed[...], jnp.concatenate(keyval_rows(1, 0) + keyval_rows(1, 1), axis=0)).astype(BF16)
        kvs1[...] = jnp.dot(squeeze[...], mixed, preferred_element_type=F32).astype(BF16)
        launch(remote(kvs1, kv1.at[lat], sem_js.at[0], sem_jr.at[lat], dev_x))
        launch(remote(kvs1, kv1.at[lat], sem_js.at[1], sem_jr.at[lat], dev_core))
        kvl[lat] = mixed

    def kv1_in(s):
        spot = kv1.at[s]
        remote(spot, spot, sem_js.at[0], sem_jr.at[s], dev_core).wait_recv()

    def share_kv1():
        kv1_in(lat_x)
        launch(remote(kv1.at[lat_x], kv1.at[lat_x], sem_js.at[2], sem_jr.at[lat_x], dev_core))

    def unfold1(s):
        kvl[s] = jnp.dot(expand[1], kv1[s], preferred_element_type=F32).astype(BF16)

    def back(k, values, s):
        lanes = pl.ds(pl.multiple_of(s * width, width), width)
        return (cur[:, lanes].astype(F32) + jnp.dot(values[...], wo[k, s], preferred_element_type=F32)).astype(BF16)

    def gathered(g):
        return lambda spot: jnp.concatenate([kvt[g, s, spot, :] for s in range(nlon)], axis=0)

    def lined(g):
        return lambda spot: jnp.concatenate(
            [kvl[s, spot, g * 128 : g * 128 + 128] for s in range(nlat)], axis=0
        )

    def norm_row(i, carry):
        spot = pl.ds(pl.multiple_of(i * STEP1, STEP1), STEP1)
        normed[spot, :] = rms(cur[spot, :].astype(F32), 1)
        return carry

    def back0():
        for s in range(nlon):
            cur[:, s * width : (s + 1) * width] = back(0, turned, s)

    def back1(s):
        lanes = pl.ds(pl.multiple_of(s * width, width), width)
        out[:, :, lanes] = back(1, att, s).reshape(cols, STEP1, width)[:, :rows, :]

    def attend0(g, low, high):
        attend(g, gathered(g), nlon * STEP0, low, high, STEP0, cols)

    def attend1(g, low, high):
        attend(g, lined(g), nlat * STEP1, low, high, STEP1, rows)

    for copy in locals_:
        copy.start()
    send_z(0, (0, 1, 2))
    for copy in hcopies:
        copy.start()
    z_in(0, 1)
    send_z(2, (0, 1, 2))
    z_in(0, 0)
    z_in(0, 2)
    send_z(1, (0, 1, 2))
    xy_in(0, 1)
    xy_in(0, 0)
    xy_in(0, 2)
    diag_in(0, 1)
    z_in(2, 0)
    diag_in(0, 0)
    z_in(2, 1)
    send_z(3, (0, 1, 2))
    whole(0, 1)
    diag_in(0, 2)
    z_in(1, 1)
    z_in(2, 2)
    whole(0, 0)
    halo_in()
    whole(0, 2)
    conv(0, 6)
    xy_in(2, 0)
    conv(6, cols)
    z_in(1, 0)
    turned[...] = jnp.dot(turn[0], normed[...], preferred_element_type=F32).astype(BF16)
    xy_in(2, 1)
    locals_[0].wait()
    send_kv0(0)
    z_in(1, 2)
    send_kv0(1)
    xy_in(1, 1)
    xy_in(1, 0)
    query_of(0, turned, 0, feature // 2)
    xy_in(2, 2)
    xy_in(1, 2)
    query_of(0, turned, feature // 2, feature)
    z_in(3, 0)
    z_in(3, 1)
    diag_in(1, 1)
    diag_in(2, 1)
    diag_in(1, 0)
    diag_in(2, 0)
    relay_kv0(0)
    kv0_in(0, 0)
    kv0_in(0, 1)
    unfold0(0)
    diag_in(2, 2)
    attend0(0, 0, rows // 2)
    attend0(0, rows // 2, rows)
    whole(2, 1)
    whole(1, 1)
    diag_in(1, 2)
    relay_kv0(1)
    whole(1, 0)
    xy_in(3, 0)
    kv0_in(1, 0)
    kv0_in(1, 1)
    unfold0(1)
    whole(2, 0)
    attend0(1, 0, rows // 2)
    xy_in(3, 1)
    attend0(1, rows // 2, rows)
    whole(1, 2)
    turned[...] = jnp.dot(turn[1], att[...], preferred_element_type=F32).astype(BF16)
    z_in(3, 2)
    locals_[1].wait()
    back0()
    lax.fori_loop(0, count // STEP1, norm_row, 0, unroll=True)
    whole(2, 2)
    locals_[2].wait()
    send_kv1()
    query_of(1, normed, 0, feature // 2)
    diag_in(3, 0)
    xy_in(3, 2)
    diag_in(3, 1)
    query_of(1, normed, feature // 2, feature)
    share_kv1()
    unfold1(lat_x)
    kv1_in(lat_core)
    unfold1(lat_core)
    whole(3, 0)
    whole(3, 1)
    diag_in(3, 2)
    kv1_in(lat_xc)
    unfold1(lat_xc)
    attend1(0, 0, 6)
    attend1(0, 6, cols)
    attend1(1, 0, 6)
    whole(3, 2)
    attend1(1, 6, cols)
    locals_[3].wait()
    back1(lon)
    back1(others[0])
    back1(others[1])
    back1(others[2])
    for copy in hcopies + pending:
        copy.wait_send()

    @pl.when(inner)
    def _():
        for m in range(4):
            at, lanes = piece(m, here)
            spot = full(m).at[0, at, lanes]
            for k in (2, 3):
                remote(spot, spot, sem_zs.at[m, k], sem_w.at[m, 0, here], dev_core).wait_send()
        for g in range(KV):
            for k in (2, 3):
                remote(kvs0.at[g], kvs0.at[g], sem_ks.at[g, k], sem_kr.at[g, 0], dev_core).wait_send()


def fused(tokens, qkv_weight, out_weight, norm_gain, conv_weight, conv_bias, nlat, nlon):
    tokens, qkv_weight = jnp.swapaxes(tokens, 0, 1), jnp.swapaxes(qkv_weight, 1, 2)
    cols, rows, feature = tokens.shape
    count = rows * STEP0
    vmem = pl.BlockSpec(memory_space=pltpu.VMEM)
    hbm = pl.BlockSpec(memory_space=pl.ANY)
    dma = pltpu.SemaphoreType.DMA
    result = pl.pallas_call(
        step_kernel,
        out_shape=jax.ShapeDtypeStruct(tokens.shape, BF16),
        in_specs=[hbm, hbm, hbm, vmem, vmem, vmem],
        out_specs=vmem,
        scratch_shapes=[
            pltpu.VMEM(tokens.shape, BF16),
            pltpu.VMEM((2, nlon) + qkv_weight.shape[1:], BF16),
            pltpu.VMEM((2, nlon) + out_weight.shape[1:], BF16),
            pltpu.VMEM((cols + 2, 40, feature), F32),
            pltpu.VMEM((2, 16, feature), F32),
            pltpu.VMEM((2, 16, feature), BF16),
            pltpu.VMEM((2, 2, 8, 128), F32),
            pltpu.VMEM((2, rows, feature), BF16),
            pltpu.VMEM((2, 16, feature), BF16),
            pltpu.VMEM((4, 8, 128), F32),
            pltpu.VMEM((count, feature), BF16),
            pltpu.VMEM((count, feature), BF16),
            pltpu.VMEM((count, feature), BF16),
            pltpu.VMEM((2, count, count), BF16),
            pltpu.VMEM((PACKED, count), BF16),
            pltpu.VMEM((2, count, PACKED), BF16),
            pltpu.VMEM((count, feature), BF16),
            pltpu.VMEM((count, feature), BF16),
            pltpu.VMEM((KV, PACKED, 2 * HD), BF16),
            pltpu.VMEM((KV, nlon, PACKED, 2 * HD), BF16),
            pltpu.VMEM((KV, nlon, count, 2 * HD), BF16),
            pltpu.VMEM((PACKED, KV * 2 * HD), BF16),
            pltpu.VMEM((nlat, PACKED, KV * 2 * HD), BF16),
            pltpu.VMEM((nlat, count, KV * 2 * HD), BF16),
            dma,
            dma((4,)),
            dma((4, 4)),
            dma((4, nlon, 4)),
            dma((4, 3, 3)),
            dma((4, 3)),
            dma((4, 3)),
            dma((8,)),
            dma((8,)),
            dma((KV, 4)),
            dma((KV, nlon)),
            dma((3,)),
            dma((nlat,)),
        ],
        compiler_params=pltpu.CompilerParams(
            collective_id=0, has_side_effects=True, vmem_limit_bytes=56 * 2**20
        ),
    )(tokens, qkv_weight, out_weight, norm_gain, conv_weight, conv_bias)
    return jnp.swapaxes(result, 0, 1)


def entry(tokens, qkv_weight, out_weight, norm_gain, conv_weight, conv_bias):
    nens, nlat, nlon = (lax.axis_size(name) for name in ("ens", "lat", "lon"))
    if (nens, nlat, nlon) == (2, 4, 4) and tokens.shape[:2] == (22, 11):
        return fused(
            tokens, qkv_weight, out_weight, norm_gain, conv_weight, conv_bias, nlat, nlon
        )
    return shards(tokens, qkv_weight, out_weight, norm_gain, conv_weight, conv_bias)


def solution(mesh):
    in_specs = (
        P(("ens", "lat"), "lon", None),
        P(None, None, "lon"),
        P(None, None, "lon"),
        P(),
        P(),
        P(),
    )
    out_specs = P(("ens", "lat"), "lon", None)
    return jax.shard_map(entry, mesh=mesh, in_specs=in_specs, out_specs=out_specs, check_vma=False)
```

```python
import functools

import jax
import jax.numpy as jnp
from jax import lax
from jax.experimental import pallas as pl
from jax.experimental.pallas import tpu as pltpu
from jax.sharding import PartitionSpec as P

HEADS = 16
KV = 2
HD = 64


def with_halo(cells, sides, width, closed):
    for axis, dim in sides:
        count = lax.axis_size(axis)
        ends = count if closed else count - 1
        head = lax.slice_in_dim(cells, 0, width, axis=dim)
        tail = lax.slice_in_dim(cells, cells.shape[dim] - width, cells.shape[dim], axis=dim)
        cells = jnp.concatenate(
            [
                lax.ppermute(tail, axis, [(i, (i + 1) % count) for i in range(ends)]),
                cells,
                lax.ppermute(head, axis, [((i + 1) % count, i) for i in range(ends)]),
            ],
            axis=dim,
        )
    return cells


def split_keyval(keyval):
    batch, length, columns = keyval.shape
    keys = keyval[..., : KV * HD].reshape(batch, length, KV, HD)
    values = keyval[..., KV * HD :].reshape(batch, length, KV, HD)
    return (keys, values)


def line_scores(query, keys):
    batch, length, feature = query.shape
    grouped = query.reshape(batch, length, KV, HEADS // KV, HD)
    return jnp.einsum(
        "nqgjd,nkgd->ngjqk", grouped, keys, preferred_element_type=jnp.float32
    ) * HD ** (-0.5)


def attend_lines(query, keyval):
    batch, length, feature = query.shape
    keys, values = split_keyval(keyval)
    scores = line_scores(query, keys)
    peak = jnp.max(scores, axis=-1, keepdims=True)
    expon = jnp.exp(scores - peak)
    denominator = jnp.sum(expon, axis=-1)
    mixed = jnp.einsum(
        "ngjqk,nkgd->nqgjd", expon.astype(jnp.bfloat16), values, preferred_element_type=jnp.float32
    )
    mixed = mixed / jnp.transpose(denominator, (0, 3, 1, 2))[..., None]
    return mixed.reshape(batch, length, feature).astype(jnp.bfloat16)


def rms_norm(current, gain):
    values = current.astype(jnp.float32)
    scaled = values * lax.rsqrt(jnp.mean(values * values, axis=-1, keepdims=True) + 1e-06)
    return (scaled * gain).astype(jnp.bfloat16)


def shards(tokens, qkv_weight, out_weight, norm_gain, conv_weight, conv_bias):
    lat_rows, lon_cols, feature = tokens.shape
    widened = with_halo(tokens, (("lon", 1),), 1, True)
    padded = with_halo(widened, (("lat", 0),), 1, False)
    total = tokens.astype(jnp.float32) + conv_bias.astype(jnp.float32)
    for shift_lat in range(3):
        for shift_lon in range(3):
            window = padded[
                shift_lat : shift_lat + lat_rows, shift_lon : shift_lon + lon_cols
            ].astype(jnp.float32)
            total = total + conv_weight[3 * shift_lat + shift_lon].astype(jnp.float32) * window
    current = total.astype(jnp.bfloat16)
    for section_index in range(2):
        weight_in, weight_out = (
            lax.all_gather(qkv_weight[section_index], "lon", axis=1, tiled=True),
            lax.all_gather(out_weight[section_index], "lon", axis=1, tiled=True),
        )
        normed = rms_norm(current, norm_gain[section_index])
        projected = jnp.dot(
            normed.reshape(-1, feature), weight_in, preferred_element_type=jnp.float32
        )
        projected = projected.astype(jnp.bfloat16).reshape(lat_rows, lon_cols, -1)
        query = projected[..., :feature]
        keyval = projected[..., feature:]
        if section_index == 0:
            gathered = lax.all_gather(keyval, "lon", axis=1, tiled=True)
            attended = attend_lines(query, gathered)
        else:
            gathered = lax.all_gather(keyval, "lat", axis=0, tiled=True)
            attended = attend_lines(
                jnp.transpose(query, (1, 0, 2)), jnp.transpose(gathered, (1, 0, 2))
            )
            attended = jnp.transpose(attended, (1, 0, 2))
        output = jnp.dot(
            attended.reshape(-1, feature), weight_out, preferred_element_type=jnp.float32
        )
        current = (
            current.astype(jnp.float32) + output.reshape(lat_rows, lon_cols, feature)
        ).astype(jnp.bfloat16)
    return current


MESH = pl.DeviceIdType.MESH
F32 = jnp.float32
BF16 = jnp.bfloat16
STEP0, STEP1, PACKED = 16, 32, 256


def remote(src, dst, send, recv, device):
    return pltpu.make_async_remote_copy(
        src_ref=src, dst_ref=dst, send_sem=send, recv_sem=recv, device_id=device, device_id_type=MESH
    )


def step_kernel(
    tokens_in, wq_in, wo_in, gain, conv_w, conv_b, out,
    tokens, wq, wo, pad, edgef, edge, corner, hcol, hrow, hcor, cur, normed, turned, turn, squeeze, expand,
    bias, held, expon, proj, att, kvs0, kv0, kvt, kvs1, kv1, kvl,
    sem_t, sem_l, sem_zs, sem_w, sem_fs, sem_c, sem_cs, sem_hs, sem_hr, sem_ks, sem_kr, sem_js, sem_jr,
):
    cols, rows, feature = tokens.shape
    nlon, nlat = 4, 4
    count = rows * STEP0
    ens, lat, lon = lax.axis_index("ens"), lax.axis_index("lat"), lax.axis_index("lon")
    xpos, core = lat // 2, lax.rem(lat, 2)

    wide = wq_in.shape[1]
    width = wo_in.shape[2]
    dev_core = (ens, 2 * xpos + 1 - core, lon)
    dev_x = (ens, 2 * (1 - xpos) + core, lon)
    dev_y = (1 - ens, lat, lon)
    here, at_x, at_y, at_xy = 2 * ens + xpos, 2 * ens + 1 - xpos, 2 * (1 - ens) + xpos, 2 * (1 - ens) + 1 - xpos
    others = (1 + lax.rem(lon, 2), lax.rem(2 + 3 * lon, 5), 3 * (1 - lon // 2))
    inner = (lon == 1) | (lon == 2)
    west, east = lax.rem(lon + 3, 4), lax.rem(lon + 1, 4)
    north, south = lax.rem(lat + 3, 4), lax.rem(lat + 1, 4)
    lat_core, lat_x, lat_xc = 2 * xpos + 1 - core, 2 * (1 - xpos) + core, 2 * (1 - xpos) + 1 - core

    barrier = pltpu.get_barrier_semaphore()
    greet = [(ens, lat, lax.rem(lon + d, 4)) for d in (1, 2, 3)]
    greet += [(ens, lax.rem(lat + d, 4), lon) for d in (1, 2, 3)]
    greet += [(ens, a, b) for a in (north, south) for b in (west, east)]
    greet += [dev_y]
    for device in greet:
        pl.semaphore_signal(barrier, inc=1, device_id=device, device_id_type=MESH)

    def piece(m, chip):
        if m % 2:
            part = width * 4 // 8
            return pl.ds(pl.multiple_of(core * (feature // 2) + chip * part, part), part), pl.ds(0, width)
        part = wide // 4
        half = feature // 2
        return pl.ds(pl.multiple_of(chip * part, 16), part), pl.ds(pl.multiple_of(core * half, half), half)

    def full(m):
        return (wo if m % 2 else wq).at[m // 2]

    def half_of(m, s, which):
        half = feature // 2
        spot = pl.ds(pl.multiple_of(which * half, half), half)
        return full(m).at[s, spot, :] if m % 2 else full(m).at[s, :, spot]

    def own(m):
        return (wo_in if m % 2 else wq_in).at[m // 2]

    load = pltpu.make_async_copy(tokens_in, tokens, sem_t)
    load.start()
    locals_ = [pltpu.make_async_copy(own(m), full(m).at[lon], sem_l.at[m]) for m in range(4)]

    cur[...] = jnp.zeros_like(cur)
    normed[...] = jnp.zeros_like(normed)

    def select(shape, index_of):
        to = lax.broadcasted_iota(jnp.int32, (shape[0], 1), 0)
        fro = lax.broadcasted_iota(jnp.int32, shape, 1)
        return jnp.where(fro == index_of(to), 1.0, 0.0).astype(BF16)

    turn[0] = select((count, count), lambda t: jnp.where(
        lax.rem(t, STEP0) < cols, lax.rem(t, STEP0) * STEP1 + t // STEP0, -1))
    turn[1] = select((count, count), lambda t: jnp.where(
        lax.rem(t, STEP1) < rows, lax.rem(t, STEP1) * STEP0 + t // STEP1, -1))
    squeeze[...] = select((PACKED, count), lambda t: jnp.where(
        t < cols * rows, (t // rows) * STEP1 + lax.rem(t, rows), -1))
    expand[0] = select((count, PACKED), lambda t: jnp.where(
        lax.rem(t, STEP0) < cols, lax.rem(t, STEP0) * rows + t // STEP0, -1))
    expand[1] = select((count, PACKED), lambda t: jnp.where(
        lax.rem(t, STEP1) < rows, (t // STEP1) * rows + lax.rem(t, STEP1), -1))

    lane = lax.broadcasted_iota(jnp.int32, bias.shape[1:], 1)
    row = lax.broadcasted_iota(jnp.int32, bias.shape[1:], 0)
    same = lax.rem(lane // STEP0, 2) == lax.rem(row // STEP0, 2)
    bias[0] = jnp.where(same & (lax.rem(lane, STEP0) < cols), 0.0, -jnp.inf)
    bias[1] = jnp.where(lax.rem(lane, STEP1) < rows, 0.0, -jnp.inf)

    load.wait()
    edgef[...] = jnp.zeros_like(edgef)
    for j in range(cols):
        line = tokens[j].astype(F32)
        pad[1 + j, 8 : 8 + rows, :] = line
        edgef[0, j : j + 1, :] = line[0:1]
        edgef[1, j : j + 1, :] = line[rows - 1 : rows]
        if j in (0, cols - 1):
            for a, r in ((0, 0), (1, rows - 1)):
                for b in range(8):
                    corner[a, j // (cols - 1), b : b + 1, :] = line[r : r + 1, 128 * b : 128 * b + 128]
    edge[...] = edgef[...].astype(BF16)

    pl.semaphore_wait(barrier, len(greet))

    pending = []

    def launch(copy):
        copy.start()
        pending.append(copy)

    def send_z(m, which=(0, 1, 2)):
        at, lanes = piece(m, here)

        def copy(k):
            return remote(
                own(m).at[at, lanes], full(m).at[lon, at, lanes],
                sem_zs.at[m, k], sem_w.at[m, lon, here], (ens, lat, others[k]),
            )

        for k in which:
            if k < 2:
                launch(copy(k))
            else:
                @pl.when(inner)
                def _():
                    copy(2).start()

    def arrived(m, s, chip):
        at, lanes = piece(m, chip)
        spot = full(m).at[s, at, lanes]
        remote(spot, spot, sem_zs.at[m, 0], sem_w.at[m, s, chip], dev_core).wait_recv()

    def pass_on(m, s, chip, send, device):
        at, lanes = piece(m, chip)
        spot = full(m).at[s, at, lanes]
        return remote(spot, spot, send, sem_w.at[m, s, chip], device)

    def z_in(m, i):
        s = others[i]
        arrived(m, s, here)
        launch(pass_on(m, s, here, sem_fs.at[m, i, 0], dev_x))
        launch(pass_on(m, s, here, sem_fs.at[m, i, 1], dev_y))
        if i == 2:
            @pl.when(inner)
            def _():
                pass_on(m, s, here, sem_zs.at[m, 3], (ens, lat, others[1])).start()

    def xy_in(m, i):
        s = others[i]
        arrived(m, s, at_x)
        if (m + i) % 2 == 0:
            launch(pass_on(m, s, at_x, sem_fs.at[m, i, 2], dev_y))
        arrived(m, s, at_y)
        if (m + i) % 2 == 1:
            launch(pass_on(m, s, at_y, sem_fs.at[m, i, 2], dev_x))

    def diag_in(m, i):
        s = others[i]
        arrived(m, s, at_xy)
        launch(remote(half_of(m, s, core), half_of(m, s, core), sem_cs.at[m, i], sem_c.at[m, i], dev_core))

    def whole(m, i):
        spot = half_of(m, others[i], 1 - core)
        remote(spot, spot, sem_cs.at[m, i], sem_c.at[m, i], dev_core).wait_recv()

    halos = [
        (tokens.at[cols - 1], hcol.at[0], (ens, lat, east)),
        (tokens.at[0], hcol.at[1], (ens, lat, west)),
        (edge.at[1], hrow.at[0], (ens, south, lon)),
        (edge.at[0], hrow.at[1], (ens, north, lon)),
        (corner.at[1, 1], hcor.at[0], (ens, south, east)),
        (corner.at[1, 0], hcor.at[1], (ens, south, west)),
        (corner.at[0, 1], hcor.at[2], (ens, north, east)),
        (corner.at[0, 0], hcor.at[3], (ens, north, west)),
    ]
    hcopies = [remote(a, b, sem_hs.at[k], sem_hr.at[k], dev) for k, (a, b, dev) in enumerate(halos)]

    def halo_in():
        for copy in hcopies:
            copy.wait_recv()
        for side, place in ((0, 0), (1, 1 + cols)):
            pad[place, 8 : 8 + rows, :] = hcol[side].astype(F32)
        for k, (spot, inside) in enumerate(((7, lat > 0), (8 + rows, lat < nlat - 1))):
            keep = jnp.where(inside, 1.0, 0.0).astype(F32)
            line = hrow[k].astype(F32) * keep
            for j in range(cols):
                pad[1 + j, spot : spot + 1, :] = line[j : j + 1]
            for b in range(8):
                lanes = slice(128 * b, 128 * b + 128)
                pad[0, spot : spot + 1, lanes] = hcor[2 * k, b : b + 1, :] * keep
                pad[1 + cols, spot : spot + 1, lanes] = hcor[2 * k + 1, b : b + 1, :] * keep

    sent = 24

    def rms(values, k):
        scaled = values * lax.rsqrt(jnp.mean(values * values, axis=-1, keepdims=True) + 1e-06)
        return (scaled * gain[k : k + 1, :]).astype(BF16)

    def conv(low, high):
        taps = conv_w[...].astype(F32)
        bias = conv_b[...].astype(F32).reshape(1, feature)
        alive = lax.broadcasted_iota(jnp.int32, (sent, 1), 0) < rows

        def conv_line(j, carry):
            total = pad[j + 1, 8 : 8 + sent, :] + bias
            for a in range(3):
                for b in range(3):
                    total = total + taps[3 * a + b : 3 * a + b + 1] * pad[j + b, 7 + a : 7 + a + sent, :]
            total = jnp.where(alive, total, 0.0)
            rounded = jnp.concatenate([total, jnp.zeros((STEP1 - sent, feature), F32)], axis=0).astype(BF16)
            spot = pl.ds(pl.multiple_of(j * STEP1, STEP1), STEP1)
            cur[spot, :] = rounded
            normed[spot, :] = rms(rounded.astype(F32), 0)
            return carry

        lax.fori_loop(low, high, conv_line, 0, unroll=True)

    def halves(block):
        left = lax.broadcasted_iota(jnp.int32, block.shape, 1) < HD
        swapped = jnp.concatenate([block[:, HD:], block[:, :HD]], axis=1)
        zero = jnp.zeros_like(block)
        keys = (jnp.where(left, block, zero), jnp.where(left, zero, swapped))
        values = (jnp.where(left, swapped, zero), jnp.where(left, zero, block))
        return keys, values

    def contract(a, b):
        return lax.dot_general(a, b, (((1,), (1,)), ((), ())), preferred_element_type=F32)

    def attend(g, block_of, low, high, which):
        pairs = HEADS // KV // 2
        span = 4 * STEP1
        sides = lax.broadcasted_iota(jnp.int32, (span, 2 * HD), 1) < HD
        ones = [jnp.where(sides, 1.0, 0.0).astype(BF16), jnp.where(sides, 0.0, 1.0).astype(BF16)]
        base = g * pairs

        def spot_of(r):
            return pl.ds(pl.multiple_of(r * STEP1, STEP1), STEP1)

        def score(r, carry):
            spot = spot_of(r)
            kh, vh = halves(block_of(spot))
            query = jnp.concatenate(
                [proj[spot, (base + p) * 128 : (base + p + 1) * 128] for p in range(pairs)], axis=0
            )
            for half in range(2):
                held[r, half] = contract(query, kh[half]) + bias[which]
            return carry

        def soften(r, carry):
            for half in range(2):
                scores = held[r, half]
                expon[r, half] = jnp.exp(scores - jnp.max(scores, axis=-1, keepdims=True)).astype(BF16)
            return carry

        def mix(r, carry):
            spot = spot_of(r)
            kh, vh = halves(block_of(spot))
            both = None
            for half in range(2):
                blend = jnp.concatenate([vh[half], ones[half]], axis=1)
                term = jnp.dot(expon[r, half], blend, preferred_element_type=F32)
                both = term if both is None else both + term
            mixed = (both[:, : 2 * HD] / both[:, 2 * HD :]).astype(BF16)
            for p in range(pairs):
                att[spot, (base + p) * 128 : (base + p + 1) * 128] = mixed[p * STEP1 : (p + 1) * STEP1]
            return carry

        for phase in (score, soften, mix):
            lax.fori_loop(low, high, phase, 0, unroll=True)

    def wide_rows(k, low, high):
        return wq.at[k].reshape(nlon * wide, feature)[low:high, :]

    def query_of(k, source, low, high):
        for t in range(low, high, 256):
            proj[:, t : t + 256] = (contract(source[...], wide_rows(k, t, t + 256)) * HD ** (-0.5)).astype(BF16)

    def keyval_rows(k, g):
        low = feature + g * HD
        return [wide_rows(k, low, low + HD), wide_rows(k, low + KV * HD, low + KV * HD + HD)]

    def send_kv0(g):
        kvs0[g] = jnp.dot(
            squeeze[...], contract(normed[...], jnp.concatenate(keyval_rows(0, g), axis=0)).astype(BF16),
            preferred_element_type=F32,
        ).astype(BF16)

        def copy(k):
            return remote(
                kvs0.at[g], kv0.at[g, lon], sem_ks.at[g, k], sem_kr.at[g, lon], (ens, lat, others[k])
            )

        launch(copy(0))
        launch(copy(1))

        @pl.when(inner)
        def _():
            copy(2).start()

        kv0[g, lon] = kvs0[g]

    def kv0_in(g, i):
        spot = kv0.at[g, others[i]]
        remote(spot, spot, sem_ks.at[g, 0], sem_kr.at[g, others[i]], dev_core).wait_recv()

    def relay_kv0(g):
        kv0_in(g, 2)

        @pl.when(inner)
        def _():
            spot = kv0.at[g, others[2]]
            remote(spot, spot, sem_ks.at[g, 3], sem_kr.at[g, others[2]], (ens, lat, others[1])).start()

    def unfold0(g):
        for s in range(nlon):
            kvt[g, s] = jnp.dot(expand[0], kv0[g, s], preferred_element_type=F32).astype(BF16)

    def send_kv1():
        mixed = contract(normed[...], jnp.concatenate(keyval_rows(1, 0) + keyval_rows(1, 1), axis=0)).astype(BF16)
        kvs1[...] = jnp.dot(squeeze[...], mixed, preferred_element_type=F32).astype(BF16)
        launch(remote(kvs1, kv1.at[lat], sem_js.at[0], sem_jr.at[lat], dev_x))
        launch(remote(kvs1, kv1.at[lat], sem_js.at[1], sem_jr.at[lat], dev_core))
        kvl[lat] = mixed

    def kv1_in(s):
        spot = kv1.at[s]
        remote(spot, spot, sem_js.at[0], sem_jr.at[s], dev_core).wait_recv()

    def share_kv1():
        kv1_in(lat_x)
        launch(remote(kv1.at[lat_x], kv1.at[lat_x], sem_js.at[2], sem_jr.at[lat_x], dev_core))

    def unfold1(s):
        kvl[s] = jnp.dot(expand[1], kv1[s], preferred_element_type=F32).astype(BF16)

    def back(k, values, s):
        lanes = pl.ds(pl.multiple_of(s * width, width), width)
        return (cur[:, lanes].astype(F32) + jnp.dot(values[...], wo[k, s], preferred_element_type=F32)).astype(BF16)

    def gathered(g):
        return lambda spot: jnp.concatenate([kvt[g, s, spot, :] for s in range(nlon)], axis=0)

    def lined(g):
        return lambda spot: jnp.concatenate(
            [kvl[s, spot, g * 128 : g * 128 + 128] for s in range(nlat)], axis=0
        )

    def norm_row(i, carry):
        spot = pl.ds(pl.multiple_of(i * STEP1, STEP1), STEP1)
        normed[spot, :] = rms(cur[spot, :].astype(F32), 1)
        return carry

    def back0():
        for s in range(nlon):
            cur[:, s * width : (s + 1) * width] = back(0, turned, s)

    def back1(s):
        lanes = pl.ds(pl.multiple_of(s * width, width), width)
        out[:, :, lanes] = back(1, att, s).reshape(cols, STEP1, width)[:, :rows, :]

    def attend0(g, low, high):
        attend(g, gathered(g), low, high, 0)

    def attend1(g, low, high):
        attend(g, lined(g), low, high, 1)

    for copy in locals_:
        copy.start()
    send_z(0, (0, 1, 2))
    for copy in hcopies:
        copy.start()
    z_in(0, 1)
    send_z(2, (0, 1, 2))
    z_in(0, 0)
    z_in(0, 2)
    send_z(1, (0, 1, 2))
    xy_in(0, 1)
    xy_in(0, 0)
    xy_in(0, 2)
    diag_in(0, 1)
    z_in(2, 0)
    diag_in(0, 0)
    z_in(2, 1)
    send_z(3, (0, 1, 2))
    whole(0, 1)
    diag_in(0, 2)
    z_in(1, 1)
    z_in(2, 2)
    whole(0, 0)
    halo_in()
    whole(0, 2)
    conv(0, 6)
    xy_in(2, 0)
    conv(6, cols)
    z_in(1, 0)
    turned[...] = jnp.dot(turn[0], normed[...], preferred_element_type=F32).astype(BF16)
    xy_in(2, 1)
    locals_[0].wait()
    send_kv0(0)
    z_in(1, 2)
    send_kv0(1)
    xy_in(1, 1)
    xy_in(1, 0)
    query_of(0, turned, 0, feature // 2)
    xy_in(2, 2)
    xy_in(1, 2)
    query_of(0, turned, feature // 2, feature)
    z_in(3, 0)
    z_in(3, 1)
    diag_in(1, 1)
    diag_in(2, 1)
    diag_in(1, 0)
    diag_in(2, 0)
    relay_kv0(0)
    kv0_in(0, 0)
    kv0_in(0, 1)
    unfold0(0)
    diag_in(2, 2)
    attend0(0, 0, 6)
    attend0(0, 6, rows // 2)
    whole(2, 1)
    whole(1, 1)
    diag_in(1, 2)
    relay_kv0(1)
    whole(1, 0)
    xy_in(3, 0)
    kv0_in(1, 0)
    kv0_in(1, 1)
    unfold0(1)
    whole(2, 0)
    attend0(1, 0, 6)
    xy_in(3, 1)
    attend0(1, 6, rows // 2)
    whole(1, 2)
    turned[...] = jnp.dot(turn[1], att[...], preferred_element_type=F32).astype(BF16)
    z_in(3, 2)
    locals_[1].wait()
    back0()
    lax.fori_loop(0, count // STEP1, norm_row, 0, unroll=True)
    whole(2, 2)
    locals_[2].wait()
    send_kv1()
    query_of(1, normed, 0, feature // 2)
    diag_in(3, 0)
    xy_in(3, 2)
    diag_in(3, 1)
    query_of(1, normed, feature // 2, feature)
    share_kv1()
    unfold1(lat_x)
    kv1_in(lat_core)
    unfold1(lat_core)
    whole(3, 0)
    whole(3, 1)
    diag_in(3, 2)
    kv1_in(lat_xc)
    unfold1(lat_xc)
    attend1(0, 0, 6)
    attend1(0, 6, cols)
    attend1(1, 0, 6)
    whole(3, 2)
    attend1(1, 6, cols)
    locals_[3].wait()
    back1(lon)
    back1(others[0])
    back1(others[1])
    back1(others[2])
    for copy in hcopies + pending:
        copy.wait_send()

    @pl.when(inner)
    def _():
        for m in range(4):
            at, lanes = piece(m, here)
            spot = full(m).at[0, at, lanes]
            for k in (2, 3):
                remote(spot, spot, sem_zs.at[m, k], sem_w.at[m, 0, here], dev_core).wait_send()
        for g in range(KV):
            for k in (2, 3):
                remote(kvs0.at[g], kvs0.at[g], sem_ks.at[g, k], sem_kr.at[g, 0], dev_core).wait_send()


def fused(tokens, qkv_weight, out_weight, norm_gain, conv_weight, conv_bias, nlat, nlon):
    tokens, qkv_weight = jnp.swapaxes(tokens, 0, 1), jnp.swapaxes(qkv_weight, 1, 2)
    cols, rows, feature = tokens.shape
    count = rows * STEP0
    vmem = pl.BlockSpec(memory_space=pltpu.VMEM)
    hbm = pl.BlockSpec(memory_space=pl.ANY)
    dma = pltpu.SemaphoreType.DMA
    result = pl.pallas_call(
        step_kernel,
        out_shape=jax.ShapeDtypeStruct(tokens.shape, BF16),
        in_specs=[hbm, hbm, hbm, vmem, vmem, vmem],
        out_specs=vmem,
        scratch_shapes=[
            pltpu.VMEM(tokens.shape, BF16),
            pltpu.VMEM((2, nlon) + qkv_weight.shape[1:], BF16),
            pltpu.VMEM((2, nlon) + out_weight.shape[1:], BF16),
            pltpu.VMEM((cols + 2, 40, feature), F32),
            pltpu.VMEM((2, 16, feature), F32),
            pltpu.VMEM((2, 16, feature), BF16),
            pltpu.VMEM((2, 2, 8, 128), F32),
            pltpu.VMEM((2, rows, feature), BF16),
            pltpu.VMEM((2, 16, feature), BF16),
            pltpu.VMEM((4, 8, 128), F32),
            pltpu.VMEM((count, feature), BF16),
            pltpu.VMEM((count, feature), BF16),
            pltpu.VMEM((count, feature), BF16),
            pltpu.VMEM((2, count, count), BF16),
            pltpu.VMEM((PACKED, count), BF16),
            pltpu.VMEM((2, count, PACKED), BF16),
            pltpu.VMEM((2, HEADS // KV // 2 * STEP1, 4 * STEP1), F32),
            pltpu.VMEM((cols, 2, HEADS // KV // 2 * STEP1, 4 * STEP1), F32),
            pltpu.VMEM((cols, 2, HEADS // KV // 2 * STEP1, 4 * STEP1), BF16),
            pltpu.VMEM((count, feature), BF16),
            pltpu.VMEM((count, feature), BF16),
            pltpu.VMEM((KV, PACKED, 2 * HD), BF16),
            pltpu.VMEM((KV, nlon, PACKED, 2 * HD), BF16),
            pltpu.VMEM((KV, nlon, count, 2 * HD), BF16),
            pltpu.VMEM((PACKED, KV * 2 * HD), BF16),
            pltpu.VMEM((nlat, PACKED, KV * 2 * HD), BF16),
            pltpu.VMEM((nlat, count, KV * 2 * HD), BF16),
            dma,
            dma((4,)),
            dma((4, 4)),
            dma((4, nlon, 4)),
            dma((4, 3, 3)),
            dma((4, 3)),
            dma((4, 3)),
            dma((8,)),
            dma((8,)),
            dma((KV, 4)),
            dma((KV, nlon)),
            dma((3,)),
            dma((nlat,)),
        ],
        compiler_params=pltpu.CompilerParams(
            collective_id=0, has_side_effects=True, vmem_limit_bytes=56 * 2**20
        ),
    )(tokens, qkv_weight, out_weight, norm_gain, conv_weight, conv_bias)
    return jnp.swapaxes(result, 0, 1)


def entry(tokens, qkv_weight, out_weight, norm_gain, conv_weight, conv_bias):
    nens, nlat, nlon = (lax.axis_size(name) for name in ("ens", "lat", "lon"))
    if (nens, nlat, nlon) == (2, 4, 4) and tokens.shape[:2] == (22, 11):
        return fused(
            tokens, qkv_weight, out_weight, norm_gain, conv_weight, conv_bias, nlat, nlon
        )
    return shards(tokens, qkv_weight, out_weight, norm_gain, conv_weight, conv_bias)


def solution(mesh):
    in_specs = (
        P(("ens", "lat"), "lon", None),
        P(None, None, "lon"),
        P(None, None, "lon"),
        P(),
        P(),
        P(),
    )
    out_specs = P(("ens", "lat"), "lon", None)
    return jax.shard_map(entry, mesh=mesh, in_specs=in_specs, out_specs=out_specs, check_vma=False)
```

```python
import functools

import jax
import jax.numpy as jnp
from jax import lax
from jax.experimental import pallas as pl
from jax.experimental.pallas import tpu as pltpu
from jax.sharding import PartitionSpec as P

HEADS = 16
KV = 2
HD = 64


def with_halo(cells, sides, width, closed):
    for axis, dim in sides:
        count = lax.axis_size(axis)
        ends = count if closed else count - 1
        head = lax.slice_in_dim(cells, 0, width, axis=dim)
        tail = lax.slice_in_dim(cells, cells.shape[dim] - width, cells.shape[dim], axis=dim)
        cells = jnp.concatenate(
            [
                lax.ppermute(tail, axis, [(i, (i + 1) % count) for i in range(ends)]),
                cells,
                lax.ppermute(head, axis, [((i + 1) % count, i) for i in range(ends)]),
            ],
            axis=dim,
        )
    return cells


def split_keyval(keyval):
    batch, length, columns = keyval.shape
    keys = keyval[..., : KV * HD].reshape(batch, length, KV, HD)
    values = keyval[..., KV * HD :].reshape(batch, length, KV, HD)
    return (keys, values)


def line_scores(query, keys):
    batch, length, feature = query.shape
    grouped = query.reshape(batch, length, KV, HEADS // KV, HD)
    return jnp.einsum(
        "nqgjd,nkgd->ngjqk", grouped, keys, preferred_element_type=jnp.float32
    ) * HD ** (-0.5)


def attend_lines(query, keyval):
    batch, length, feature = query.shape
    keys, values = split_keyval(keyval)
    scores = line_scores(query, keys)
    peak = jnp.max(scores, axis=-1, keepdims=True)
    expon = jnp.exp(scores - peak)
    denominator = jnp.sum(expon, axis=-1)
    mixed = jnp.einsum(
        "ngjqk,nkgd->nqgjd", expon.astype(jnp.bfloat16), values, preferred_element_type=jnp.float32
    )
    mixed = mixed / jnp.transpose(denominator, (0, 3, 1, 2))[..., None]
    return mixed.reshape(batch, length, feature).astype(jnp.bfloat16)


def rms_norm(current, gain):
    values = current.astype(jnp.float32)
    scaled = values * lax.rsqrt(jnp.mean(values * values, axis=-1, keepdims=True) + 1e-06)
    return (scaled * gain).astype(jnp.bfloat16)


def shards(tokens, qkv_weight, out_weight, norm_gain, conv_weight, conv_bias):
    lat_rows, lon_cols, feature = tokens.shape
    widened = with_halo(tokens, (("lon", 1),), 1, True)
    padded = with_halo(widened, (("lat", 0),), 1, False)
    total = tokens.astype(jnp.float32) + conv_bias.astype(jnp.float32)
    for shift_lat in range(3):
        for shift_lon in range(3):
            window = padded[
                shift_lat : shift_lat + lat_rows, shift_lon : shift_lon + lon_cols
            ].astype(jnp.float32)
            total = total + conv_weight[3 * shift_lat + shift_lon].astype(jnp.float32) * window
    current = total.astype(jnp.bfloat16)
    for section_index in range(2):
        weight_in, weight_out = (
            lax.all_gather(qkv_weight[section_index], "lon", axis=1, tiled=True),
            lax.all_gather(out_weight[section_index], "lon", axis=1, tiled=True),
        )
        normed = rms_norm(current, norm_gain[section_index])
        projected = jnp.dot(
            normed.reshape(-1, feature), weight_in, preferred_element_type=jnp.float32
        )
        projected = projected.astype(jnp.bfloat16).reshape(lat_rows, lon_cols, -1)
        query = projected[..., :feature]
        keyval = projected[..., feature:]
        if section_index == 0:
            gathered = lax.all_gather(keyval, "lon", axis=1, tiled=True)
            attended = attend_lines(query, gathered)
        else:
            gathered = lax.all_gather(keyval, "lat", axis=0, tiled=True)
            attended = attend_lines(
                jnp.transpose(query, (1, 0, 2)), jnp.transpose(gathered, (1, 0, 2))
            )
            attended = jnp.transpose(attended, (1, 0, 2))
        output = jnp.dot(
            attended.reshape(-1, feature), weight_out, preferred_element_type=jnp.float32
        )
        current = (
            current.astype(jnp.float32) + output.reshape(lat_rows, lon_cols, feature)
        ).astype(jnp.bfloat16)
    return current


MESH = pl.DeviceIdType.MESH
F32 = jnp.float32
BF16 = jnp.bfloat16
STEP0, STEP1, PACKED = 16, 32, 256


def remote(src, dst, send, recv, device):
    return pltpu.make_async_remote_copy(
        src_ref=src, dst_ref=dst, send_sem=send, recv_sem=recv, device_id=device, device_id_type=MESH
    )


def step_kernel(
    tokens_in, wq_in, wo_in, gain, conv_w, conv_b, out,
    tokens, wq, wo, pad, edgef, edge, corner, hcol, hrow, hcor, cur, normed, turned, turn, squeeze, expand,
    bias, held, expon, proj, att, kvs0, kv0, kvt, kvs1, kv1, kvl,
    sem_t, sem_l, sem_zs, sem_w, sem_fs, sem_c, sem_cs, sem_hs, sem_hr, sem_ks, sem_kr, sem_js, sem_jr,
):
    cols, rows, feature = tokens.shape
    nlon, nlat = 4, 4
    count = rows * STEP0
    ens, lat, lon = lax.axis_index("ens"), lax.axis_index("lat"), lax.axis_index("lon")
    xpos, core = lat // 2, lax.rem(lat, 2)

    wide = wq_in.shape[1]
    width = wo_in.shape[2]
    dev_core = (ens, 2 * xpos + 1 - core, lon)
    dev_x = (ens, 2 * (1 - xpos) + core, lon)
    dev_y = (1 - ens, lat, lon)
    here, at_x, at_y, at_xy = 2 * ens + xpos, 2 * ens + 1 - xpos, 2 * (1 - ens) + xpos, 2 * (1 - ens) + 1 - xpos
    others = (1 + lax.rem(lon, 2), lax.rem(2 + 3 * lon, 5), 3 * (1 - lon // 2))
    inner = (lon == 1) | (lon == 2)
    west, east = lax.rem(lon + 3, 4), lax.rem(lon + 1, 4)
    north, south = lax.rem(lat + 3, 4), lax.rem(lat + 1, 4)
    lat_core, lat_x, lat_xc = 2 * xpos + 1 - core, 2 * (1 - xpos) + core, 2 * (1 - xpos) + 1 - core

    barrier = pltpu.get_barrier_semaphore()
    greet = [(ens, lat, lax.rem(lon + d, 4)) for d in (1, 2, 3)]
    greet += [(ens, lax.rem(lat + d, 4), lon) for d in (1, 2, 3)]
    greet += [(ens, a, b) for a in (north, south) for b in (west, east)]
    greet += [dev_y]
    for device in greet:
        pl.semaphore_signal(barrier, inc=1, device_id=device, device_id_type=MESH)

    def piece(m, chip):
        if m % 2:
            part = width * 4 // 8
            return pl.ds(pl.multiple_of(core * (feature // 2) + chip * part, part), part), pl.ds(0, width)
        part = wide // 4
        half = feature // 2
        return pl.ds(pl.multiple_of(chip * part, 16), part), pl.ds(pl.multiple_of(core * half, half), half)

    def full(m):
        return (wo if m % 2 else wq).at[m // 2]

    def half_of(m, s, which):
        half = feature // 2
        spot = pl.ds(pl.multiple_of(which * half, half), half)
        return full(m).at[s, spot, :] if m % 2 else full(m).at[s, :, spot]

    def own(m):
        return (wo_in if m % 2 else wq_in).at[m // 2]

    load = pltpu.make_async_copy(tokens_in, tokens, sem_t)
    load.start()
    locals_ = [pltpu.make_async_copy(own(m), full(m).at[lon], sem_l.at[m]) for m in range(4)]

    cur[...] = jnp.zeros_like(cur)
    normed[...] = jnp.zeros_like(normed)

    def select(shape, index_of):
        to = lax.broadcasted_iota(jnp.int32, (shape[0], 1), 0)
        fro = lax.broadcasted_iota(jnp.int32, shape, 1)
        return jnp.where(fro == index_of(to), 1.0, 0.0).astype(BF16)

    turn[0] = select((count, count), lambda t: jnp.where(
        lax.rem(t, STEP0) < cols, lax.rem(t, STEP0) * STEP1 + t // STEP0, -1))
    turn[1] = select((count, count), lambda t: jnp.where(
        lax.rem(t, STEP1) < rows, lax.rem(t, STEP1) * STEP0 + t // STEP1, -1))
    squeeze[...] = select((PACKED, count), lambda t: jnp.where(
        t < cols * rows, (t // rows) * STEP1 + lax.rem(t, rows), -1))
    expand[0] = select((count, PACKED), lambda t: jnp.where(
        lax.rem(t, STEP0) < cols, lax.rem(t, STEP0) * rows + t // STEP0, -1))
    expand[1] = select((count, PACKED), lambda t: jnp.where(
        lax.rem(t, STEP1) < rows, (t // STEP1) * rows + lax.rem(t, STEP1), -1))

    lane = lax.broadcasted_iota(jnp.int32, bias.shape[1:], 1)
    row = lax.broadcasted_iota(jnp.int32, bias.shape[1:], 0)
    same = lax.rem(lane // STEP0, 2) == lax.rem(row // STEP0, 2)
    bias[0] = jnp.where(same & (lax.rem(lane, STEP0) < cols), 0.0, -jnp.inf)
    bias[1] = jnp.where(lax.rem(lane, STEP1) < rows, 0.0, -jnp.inf)

    load.wait()
    edgef[...] = jnp.zeros_like(edgef)
    for j in range(cols):
        line = tokens[j].astype(F32)
        pad[1 + j, 8 : 8 + rows, :] = line
        edgef[0, j : j + 1, :] = line[0:1]
        edgef[1, j : j + 1, :] = line[rows - 1 : rows]
        if j in (0, cols - 1):
            for a, r in ((0, 0), (1, rows - 1)):
                for b in range(8):
                    corner[a, j // (cols - 1), b : b + 1, :] = line[r : r + 1, 128 * b : 128 * b + 128]
    edge[...] = edgef[...].astype(BF16)

    pl.semaphore_wait(barrier, len(greet))

    pending = []

    def launch(copy):
        copy.start()
        pending.append(copy)

    def send_z(m, which=(0, 1, 2)):
        at, lanes = piece(m, here)

        def copy(k):
            return remote(
                own(m).at[at, lanes], full(m).at[lon, at, lanes],
                sem_zs.at[m, k], sem_w.at[m, lon, here], (ens, lat, others[k]),
            )

        for k in which:
            if k < 2:
                launch(copy(k))
            else:
                @pl.when(inner)
                def _():
                    copy(2).start()

    def arrived(m, s, chip):
        at, lanes = piece(m, chip)
        spot = full(m).at[s, at, lanes]
        remote(spot, spot, sem_zs.at[m, 0], sem_w.at[m, s, chip], dev_core).wait_recv()

    def pass_on(m, s, chip, send, device):
        at, lanes = piece(m, chip)
        spot = full(m).at[s, at, lanes]
        return remote(spot, spot, send, sem_w.at[m, s, chip], device)

    def z_in(m, i):
        s = others[i]
        arrived(m, s, here)
        launch(pass_on(m, s, here, sem_fs.at[m, i, 0], dev_x))
        launch(pass_on(m, s, here, sem_fs.at[m, i, 1], dev_y))
        if i == 2:
            @pl.when(inner)
            def _():
                pass_on(m, s, here, sem_zs.at[m, 3], (ens, lat, others[1])).start()

    def xy_in(m, i):
        s = others[i]
        arrived(m, s, at_x)
        if (m + i) % 2 == 0:
            launch(pass_on(m, s, at_x, sem_fs.at[m, i, 2], dev_y))
        arrived(m, s, at_y)
        if (m + i) % 2 == 1:
            launch(pass_on(m, s, at_y, sem_fs.at[m, i, 2], dev_x))

    def diag_in(m, i):
        s = others[i]
        arrived(m, s, at_xy)
        launch(remote(half_of(m, s, core), half_of(m, s, core), sem_cs.at[m, i], sem_c.at[m, i], dev_core))

    def whole(m, i):
        spot = half_of(m, others[i], 1 - core)
        remote(spot, spot, sem_cs.at[m, i], sem_c.at[m, i], dev_core).wait_recv()

    halos = [
        (tokens.at[cols - 1], hcol.at[0], (ens, lat, east)),
        (tokens.at[0], hcol.at[1], (ens, lat, west)),
        (edge.at[1], hrow.at[0], (ens, south, lon)),
        (edge.at[0], hrow.at[1], (ens, north, lon)),
        (corner.at[1, 1], hcor.at[0], (ens, south, east)),
        (corner.at[1, 0], hcor.at[1], (ens, south, west)),
        (corner.at[0, 1], hcor.at[2], (ens, north, east)),
        (corner.at[0, 0], hcor.at[3], (ens, north, west)),
    ]
    hcopies = [remote(a, b, sem_hs.at[k], sem_hr.at[k], dev) for k, (a, b, dev) in enumerate(halos)]

    def halo_in():
        for copy in hcopies:
            copy.wait_recv()
        for side, place in ((0, 0), (1, 1 + cols)):
            pad[place, 8 : 8 + rows, :] = hcol[side].astype(F32)
        for k, (spot, inside) in enumerate(((7, lat > 0), (8 + rows, lat < nlat - 1))):
            keep = jnp.where(inside, 1.0, 0.0).astype(F32)
            line = hrow[k].astype(F32) * keep
            for j in range(cols):
                pad[1 + j, spot : spot + 1, :] = line[j : j + 1]
            for b in range(8):
                lanes = slice(128 * b, 128 * b + 128)
                pad[0, spot : spot + 1, lanes] = hcor[2 * k, b : b + 1, :] * keep
                pad[1 + cols, spot : spot + 1, lanes] = hcor[2 * k + 1, b : b + 1, :] * keep

    sent = 24

    def rms(values, k):
        scaled = values * lax.rsqrt(jnp.mean(values * values, axis=-1, keepdims=True) + 1e-06)
        return (scaled * gain[k : k + 1, :]).astype(BF16)

    def conv(low, high):
        taps = conv_w[...].astype(F32)
        bias = conv_b[...].astype(F32).reshape(1, feature)
        alive = lax.broadcasted_iota(jnp.int32, (sent, 1), 0) < rows

        def conv_line(j, carry):
            total = pad[j + 1, 8 : 8 + sent, :] + bias
            for a in range(3):
                for b in range(3):
                    total = total + taps[3 * a + b : 3 * a + b + 1] * pad[j + b, 7 + a : 7 + a + sent, :]
            total = jnp.where(alive, total, 0.0)
            rounded = jnp.concatenate([total, jnp.zeros((STEP1 - sent, feature), F32)], axis=0).astype(BF16)
            spot = pl.ds(pl.multiple_of(j * STEP1, STEP1), STEP1)
            cur[spot, :] = rounded
            normed[spot, :] = rms(rounded.astype(F32), 0)
            return carry

        lax.fori_loop(low, high, conv_line, 0, unroll=True)

    def halves(block):
        left = lax.broadcasted_iota(jnp.int32, block.shape, 1) < HD
        swapped = jnp.concatenate([block[:, HD:], block[:, :HD]], axis=1)
        zero = jnp.zeros_like(block)
        keys = (jnp.where(left, block, zero), jnp.where(left, zero, swapped))
        values = (jnp.where(left, swapped, zero), jnp.where(left, zero, block))
        return keys, values

    def contract(a, b):
        return lax.dot_general(a, b, (((1,), (1,)), ((), ())), preferred_element_type=F32)

    def attend(g, block_of, low, high, which):
        pairs = HEADS // KV // 2
        span = 4 * STEP1
        sides = lax.broadcasted_iota(jnp.int32, (span, 2 * HD), 1) < HD
        ones = [jnp.where(sides, 1.0, 0.0).astype(BF16), jnp.where(sides, 0.0, 1.0).astype(BF16)]
        base = g * pairs

        def spot_of(r):
            return pl.ds(pl.multiple_of(r * STEP1, STEP1), STEP1)

        def score(r, carry):
            spot = spot_of(r)
            kh, vh = halves(block_of(spot))
            query = jnp.concatenate(
                [proj[spot, (base + p) * 128 : (base + p + 1) * 128] for p in range(pairs)], axis=0
            )
            for half in range(2):
                held[r, half] = contract(query, kh[half]) + bias[which]
            return carry

        def soften(r, carry):
            for half in range(2):
                scores = held[r, half]
                expon[r, half] = jnp.exp(scores - jnp.max(scores, axis=-1, keepdims=True)).astype(BF16)
            return carry

        def mix(r, carry):
            spot = spot_of(r)
            kh, vh = halves(block_of(spot))
            both = None
            for half in range(2):
                blend = jnp.concatenate([vh[half], ones[half]], axis=1)
                term = jnp.dot(expon[r, half], blend, preferred_element_type=F32)
                both = term if both is None else both + term
            mixed = (both[:, : 2 * HD] / both[:, 2 * HD :]).astype(BF16)
            for p in range(pairs):
                att[spot, (base + p) * 128 : (base + p + 1) * 128] = mixed[p * STEP1 : (p + 1) * STEP1]
            return carry

        for phase in (score, soften, mix):
            lax.fori_loop(low, high, phase, 0, unroll=True)

    def wide_rows(k, low, high):
        return wq.at[k].reshape(nlon * wide, feature)[low:high, :]

    def query_of(k, source, low, high):
        for t in range(low, high, 256):
            proj[:, t : t + 256] = (contract(source[...], wide_rows(k, t, t + 256)) * HD ** (-0.5)).astype(BF16)

    def keyval_rows(k, g):
        low = feature + g * HD
        return [wide_rows(k, low, low + HD), wide_rows(k, low + KV * HD, low + KV * HD + HD)]

    def send_kv0(g):
        kvs0[g] = jnp.dot(
            squeeze[...], contract(normed[...], jnp.concatenate(keyval_rows(0, g), axis=0)).astype(BF16),
            preferred_element_type=F32,
        ).astype(BF16)

        def copy(k):
            return remote(
                kvs0.at[g], kv0.at[g, lon], sem_ks.at[g, k], sem_kr.at[g, lon], (ens, lat, others[k])
            )

        launch(copy(0))
        launch(copy(1))

        @pl.when(inner)
        def _():
            copy(2).start()

        kv0[g, lon] = kvs0[g]

    def kv0_in(g, i):
        spot = kv0.at[g, others[i]]
        remote(spot, spot, sem_ks.at[g, 0], sem_kr.at[g, others[i]], dev_core).wait_recv()

    def relay_kv0(g):
        kv0_in(g, 2)

        @pl.when(inner)
        def _():
            spot = kv0.at[g, others[2]]
            remote(spot, spot, sem_ks.at[g, 3], sem_kr.at[g, others[2]], (ens, lat, others[1])).start()

    def unfold0(g):
        for s in range(nlon):
            kvt[g, s] = jnp.dot(expand[0], kv0[g, s], preferred_element_type=F32).astype(BF16)

    def send_kv1():
        mixed = contract(normed[...], jnp.concatenate(keyval_rows(1, 0) + keyval_rows(1, 1), axis=0)).astype(BF16)
        kvs1[...] = jnp.dot(squeeze[...], mixed, preferred_element_type=F32).astype(BF16)
        launch(remote(kvs1, kv1.at[lat], sem_js.at[0], sem_jr.at[lat], dev_x))
        launch(remote(kvs1, kv1.at[lat], sem_js.at[1], sem_jr.at[lat], dev_core))
        kvl[lat] = mixed

    def kv1_in(s):
        spot = kv1.at[s]
        remote(spot, spot, sem_js.at[0], sem_jr.at[s], dev_core).wait_recv()

    def share_kv1():
        kv1_in(lat_x)
        launch(remote(kv1.at[lat_x], kv1.at[lat_x], sem_js.at[2], sem_jr.at[lat_x], dev_core))

    def unfold1(s):
        kvl[s] = jnp.dot(expand[1], kv1[s], preferred_element_type=F32).astype(BF16)

    def back(k, values, s):
        lanes = pl.ds(pl.multiple_of(s * width, width), width)
        return (cur[:, lanes].astype(F32) + jnp.dot(values[...], wo[k, s], preferred_element_type=F32)).astype(BF16)

    def gathered(g):
        return lambda spot: jnp.concatenate([kvt[g, s, spot, :] for s in range(nlon)], axis=0)

    def lined(g):
        return lambda spot: jnp.concatenate(
            [kvl[s, spot, g * 128 : g * 128 + 128] for s in range(nlat)], axis=0
        )

    def norm_row(i, carry):
        spot = pl.ds(pl.multiple_of(i * STEP1, STEP1), STEP1)
        normed[spot, :] = rms(cur[spot, :].astype(F32), 1)
        return carry

    def back0():
        for s in range(nlon):
            cur[:, s * width : (s + 1) * width] = back(0, turned, s)

    def back1(s):
        lanes = pl.ds(pl.multiple_of(s * width, width), width)
        out[:, :, lanes] = back(1, att, s).reshape(cols, STEP1, width)[:, :rows, :]

    def attend0(g, low, high):
        attend(g, gathered(g), low, high, 0)

    def attend1(g, low, high):
        attend(g, lined(g), low, high, 1)

    for copy in locals_:
        copy.start()
    send_z(0, (0, 1, 2))
    for copy in hcopies:
        copy.start()
    z_in(0, 0)
    z_in(0, 1)
    send_z(2, (0, 1, 2))
    z_in(0, 2)
    send_z(1, (0, 1, 2))
    xy_in(0, 1)
    xy_in(0, 0)
    xy_in(0, 2)
    z_in(2, 1)
    diag_in(0, 0)
    z_in(2, 0)
    send_z(3, (0, 1, 2))
    diag_in(0, 2)
    halo_in()
    z_in(1, 1)
    whole(0, 0)
    z_in(2, 2)
    conv(0, 6)
    diag_in(0, 1)
    z_in(1, 0)
    whole(0, 2)
    conv(6, cols)
    z_in(1, 2)
    turned[...] = jnp.dot(turn[0], normed[...], preferred_element_type=F32).astype(BF16)
    xy_in(2, 0)
    whole(0, 1)
    locals_[0].wait()
    send_kv0(0)
    xy_in(2, 1)
    send_kv0(1)
    xy_in(1, 0)
    query_of(0, turned, 0, feature // 2)
    xy_in(1, 2)
    xy_in(1, 1)
    query_of(0, turned, feature // 2, feature)
    xy_in(2, 2)
    z_in(3, 2)
    diag_in(1, 0)
    z_in(3, 0)
    relay_kv0(0)
    diag_in(1, 1)
    kv0_in(0, 0)
    kv0_in(0, 1)
    unfold0(0)
    diag_in(1, 2)
    attend0(0, 0, 6)
    attend0(0, 6, rows // 2)
    diag_in(2, 0)
    diag_in(2, 1)
    relay_kv0(1)
    kv0_in(1, 0)
    kv0_in(1, 1)
    whole(1, 1)
    unfold0(1)
    diag_in(2, 2)
    z_in(3, 1)
    attend0(1, 0, 6)
    xy_in(3, 0)
    whole(1, 2)
    attend0(1, 6, rows // 2)
    whole(1, 0)
    turned[...] = jnp.dot(turn[1], att[...], preferred_element_type=F32).astype(BF16)
    whole(2, 0)
    locals_[1].wait()
    back0()
    lax.fori_loop(0, count // STEP1, norm_row, 0, unroll=True)
    whole(2, 2)
    whole(2, 1)
    locals_[2].wait()
    send_kv1()
    xy_in(3, 1)
    xy_in(3, 2)
    query_of(1, normed, 0, feature // 2)
    query_of(1, normed, feature // 2, feature)
    diag_in(3, 1)
    share_kv1()
    unfold1(lat_x)
    kv1_in(lat_core)
    unfold1(lat_core)
    diag_in(3, 0)
    diag_in(3, 2)
    kv1_in(lat_xc)
    unfold1(lat_xc)
    attend1(0, 0, 6)
    attend1(0, 6, cols)
    attend1(1, 0, 6)
    whole(3, 0)
    attend1(1, 6, cols)
    locals_[3].wait()
    back1(lon)
    back1(others[0])
    whole(3, 2)
    whole(3, 1)
    back1(others[1])
    back1(others[2])
    for copy in hcopies + pending:
        copy.wait_send()

    @pl.when(inner)
    def _():
        for m in range(4):
            at, lanes = piece(m, here)
            spot = full(m).at[0, at, lanes]
            for k in (2, 3):
                remote(spot, spot, sem_zs.at[m, k], sem_w.at[m, 0, here], dev_core).wait_send()
        for g in range(KV):
            for k in (2, 3):
                remote(kvs0.at[g], kvs0.at[g], sem_ks.at[g, k], sem_kr.at[g, 0], dev_core).wait_send()


def fused(tokens, qkv_weight, out_weight, norm_gain, conv_weight, conv_bias, nlat, nlon):
    tokens, qkv_weight = jnp.swapaxes(tokens, 0, 1), jnp.swapaxes(qkv_weight, 1, 2)
    cols, rows, feature = tokens.shape
    count = rows * STEP0
    vmem = pl.BlockSpec(memory_space=pltpu.VMEM)
    hbm = pl.BlockSpec(memory_space=pl.ANY)
    dma = pltpu.SemaphoreType.DMA
    result = pl.pallas_call(
        step_kernel,
        out_shape=jax.ShapeDtypeStruct(tokens.shape, BF16),
        in_specs=[hbm, hbm, hbm, vmem, vmem, vmem],
        out_specs=vmem,
        scratch_shapes=[
            pltpu.VMEM(tokens.shape, BF16),
            pltpu.VMEM((2, nlon) + qkv_weight.shape[1:], BF16),
            pltpu.VMEM((2, nlon) + out_weight.shape[1:], BF16),
            pltpu.VMEM((cols + 2, 40, feature), F32),
            pltpu.VMEM((2, 16, feature), F32),
            pltpu.VMEM((2, 16, feature), BF16),
            pltpu.VMEM((2, 2, 8, 128), F32),
            pltpu.VMEM((2, rows, feature), BF16),
            pltpu.VMEM((2, 16, feature), BF16),
            pltpu.VMEM((4, 8, 128), F32),
            pltpu.VMEM((count, feature), BF16),
            pltpu.VMEM((count, feature), BF16),
            pltpu.VMEM((count, feature), BF16),
            pltpu.VMEM((2, count, count), BF16),
            pltpu.VMEM((PACKED, count), BF16),
            pltpu.VMEM((2, count, PACKED), BF16),
            pltpu.VMEM((2, HEADS // KV // 2 * STEP1, 4 * STEP1), F32),
            pltpu.VMEM((cols, 2, HEADS // KV // 2 * STEP1, 4 * STEP1), F32),
            pltpu.VMEM((cols, 2, HEADS // KV // 2 * STEP1, 4 * STEP1), BF16),
            pltpu.VMEM((count, feature), BF16),
            pltpu.VMEM((count, feature), BF16),
            pltpu.VMEM((KV, PACKED, 2 * HD), BF16),
            pltpu.VMEM((KV, nlon, PACKED, 2 * HD), BF16),
            pltpu.VMEM((KV, nlon, count, 2 * HD), BF16),
            pltpu.VMEM((PACKED, KV * 2 * HD), BF16),
            pltpu.VMEM((nlat, PACKED, KV * 2 * HD), BF16),
            pltpu.VMEM((nlat, count, KV * 2 * HD), BF16),
            dma,
            dma((4,)),
            dma((4, 4)),
            dma((4, nlon, 4)),
            dma((4, 3, 3)),
            dma((4, 3)),
            dma((4, 3)),
            dma((8,)),
            dma((8,)),
            dma((KV, 4)),
            dma((KV, nlon)),
            dma((3,)),
            dma((nlat,)),
        ],
        compiler_params=pltpu.CompilerParams(
            collective_id=0, has_side_effects=True, vmem_limit_bytes=56 * 2**20
        ),
    )(tokens, qkv_weight, out_weight, norm_gain, conv_weight, conv_bias)
    return jnp.swapaxes(result, 0, 1)


def entry(tokens, qkv_weight, out_weight, norm_gain, conv_weight, conv_bias):
    nens, nlat, nlon = (lax.axis_size(name) for name in ("ens", "lat", "lon"))
    if (nens, nlat, nlon) == (2, 4, 4) and tokens.shape[:2] == (22, 11):
        return fused(
            tokens, qkv_weight, out_weight, norm_gain, conv_weight, conv_bias, nlat, nlon
        )
    return shards(tokens, qkv_weight, out_weight, norm_gain, conv_weight, conv_bias)


def solution(mesh):
    in_specs = (
        P(("ens", "lat"), "lon", None),
        P(None, None, "lon"),
        P(None, None, "lon"),
        P(),
        P(),
        P(),
    )
    out_specs = P(("ens", "lat"), "lon", None)
    return jax.shard_map(entry, mesh=mesh, in_specs=in_specs, out_specs=out_specs, check_vma=False)
```

```python
import functools

import jax
import jax.numpy as jnp
from jax import lax
from jax.experimental import pallas as pl
from jax.experimental.pallas import tpu as pltpu
from jax.sharding import PartitionSpec as P

HEADS = 16
KV = 2
HD = 64


def with_halo(cells, sides, width, closed):
    for axis, dim in sides:
        count = lax.axis_size(axis)
        ends = count if closed else count - 1
        head = lax.slice_in_dim(cells, 0, width, axis=dim)
        tail = lax.slice_in_dim(cells, cells.shape[dim] - width, cells.shape[dim], axis=dim)
        cells = jnp.concatenate(
            [
                lax.ppermute(tail, axis, [(i, (i + 1) % count) for i in range(ends)]),
                cells,
                lax.ppermute(head, axis, [((i + 1) % count, i) for i in range(ends)]),
            ],
            axis=dim,
        )
    return cells


def split_keyval(keyval):
    batch, length, columns = keyval.shape
    keys = keyval[..., : KV * HD].reshape(batch, length, KV, HD)
    values = keyval[..., KV * HD :].reshape(batch, length, KV, HD)
    return (keys, values)


def line_scores(query, keys):
    batch, length, feature = query.shape
    grouped = query.reshape(batch, length, KV, HEADS // KV, HD)
    return jnp.einsum(
        "nqgjd,nkgd->ngjqk", grouped, keys, preferred_element_type=jnp.float32
    ) * HD ** (-0.5)


def attend_lines(query, keyval):
    batch, length, feature = query.shape
    keys, values = split_keyval(keyval)
    scores = line_scores(query, keys)
    peak = jnp.max(scores, axis=-1, keepdims=True)
    expon = jnp.exp(scores - peak)
    denominator = jnp.sum(expon, axis=-1)
    mixed = jnp.einsum(
        "ngjqk,nkgd->nqgjd", expon.astype(jnp.bfloat16), values, preferred_element_type=jnp.float32
    )
    mixed = mixed / jnp.transpose(denominator, (0, 3, 1, 2))[..., None]
    return mixed.reshape(batch, length, feature).astype(jnp.bfloat16)


def rms_norm(current, gain):
    values = current.astype(jnp.float32)
    scaled = values * lax.rsqrt(jnp.mean(values * values, axis=-1, keepdims=True) + 1e-06)
    return (scaled * gain).astype(jnp.bfloat16)


def shards(tokens, qkv_weight, out_weight, norm_gain, conv_weight, conv_bias):
    lat_rows, lon_cols, feature = tokens.shape
    widened = with_halo(tokens, (("lon", 1),), 1, True)
    padded = with_halo(widened, (("lat", 0),), 1, False)
    total = tokens.astype(jnp.float32) + conv_bias.astype(jnp.float32)
    for shift_lat in range(3):
        for shift_lon in range(3):
            window = padded[
                shift_lat : shift_lat + lat_rows, shift_lon : shift_lon + lon_cols
            ].astype(jnp.float32)
            total = total + conv_weight[3 * shift_lat + shift_lon].astype(jnp.float32) * window
    current = total.astype(jnp.bfloat16)
    for section_index in range(2):
        weight_in, weight_out = (
            lax.all_gather(qkv_weight[section_index], "lon", axis=1, tiled=True),
            lax.all_gather(out_weight[section_index], "lon", axis=1, tiled=True),
        )
        normed = rms_norm(current, norm_gain[section_index])
        projected = jnp.dot(
            normed.reshape(-1, feature), weight_in, preferred_element_type=jnp.float32
        )
        projected = projected.astype(jnp.bfloat16).reshape(lat_rows, lon_cols, -1)
        query = projected[..., :feature]
        keyval = projected[..., feature:]
        if section_index == 0:
            gathered = lax.all_gather(keyval, "lon", axis=1, tiled=True)
            attended = attend_lines(query, gathered)
        else:
            gathered = lax.all_gather(keyval, "lat", axis=0, tiled=True)
            attended = attend_lines(
                jnp.transpose(query, (1, 0, 2)), jnp.transpose(gathered, (1, 0, 2))
            )
            attended = jnp.transpose(attended, (1, 0, 2))
        output = jnp.dot(
            attended.reshape(-1, feature), weight_out, preferred_element_type=jnp.float32
        )
        current = (
            current.astype(jnp.float32) + output.reshape(lat_rows, lon_cols, feature)
        ).astype(jnp.bfloat16)
    return current


MESH = pl.DeviceIdType.MESH
F32 = jnp.float32
BF16 = jnp.bfloat16
STEP0, STEP1, PACKED = 16, 32, 256


def remote(src, dst, send, recv, device):
    return pltpu.make_async_remote_copy(
        src_ref=src, dst_ref=dst, send_sem=send, recv_sem=recv, device_id=device, device_id_type=MESH
    )


def step_kernel(
    tokens_in, wq_in, wo_in, gain, conv_w, conv_b, out,
    tokens, wq, wo, pad, edgef, edge, corner, hcol, hrow, hcor, cur, normed, turned, turn, squeeze, expand,
    bias, held, expon, proj, att, kvs0, kv0, kvt, kvs1, kv1, kvl,
    sem_t, sem_l, sem_zs, sem_w, sem_fs, sem_c, sem_cs, sem_hs, sem_hr, sem_ks, sem_kr, sem_js, sem_jr,
):
    cols, rows, feature = tokens.shape
    nlon, nlat = 4, 4
    count = rows * STEP0
    ens, lat, lon = lax.axis_index("ens"), lax.axis_index("lat"), lax.axis_index("lon")
    xpos, core = lat // 2, lax.rem(lat, 2)

    wide = wq_in.shape[1]
    width = wo_in.shape[2]
    dev_core = (ens, 2 * xpos + 1 - core, lon)
    dev_x = (ens, 2 * (1 - xpos) + core, lon)
    dev_y = (1 - ens, lat, lon)
    here, at_x, at_y, at_xy = 2 * ens + xpos, 2 * ens + 1 - xpos, 2 * (1 - ens) + xpos, 2 * (1 - ens) + 1 - xpos
    others = (1 + lax.rem(lon, 2), lax.rem(2 + 3 * lon, 5), 3 * (1 - lon // 2))
    inner = (lon == 1) | (lon == 2)
    west, east = lax.rem(lon + 3, 4), lax.rem(lon + 1, 4)
    north, south = lax.rem(lat + 3, 4), lax.rem(lat + 1, 4)
    lat_core, lat_x, lat_xc = 2 * xpos + 1 - core, 2 * (1 - xpos) + core, 2 * (1 - xpos) + 1 - core

    barrier = pltpu.get_barrier_semaphore()
    greet = [(ens, lat, lax.rem(lon + d, 4)) for d in (1, 2, 3)]
    greet += [(ens, lax.rem(lat + d, 4), lon) for d in (1, 2, 3)]
    greet += [(ens, a, b) for a in (north, south) for b in (west, east)]
    greet += [dev_y]
    for device in greet:
        pl.semaphore_signal(barrier, inc=1, device_id=device, device_id_type=MESH)

    def piece(m, chip):
        if m % 2:
            part = width * 4 // 8
            return pl.ds(pl.multiple_of(core * (feature // 2) + chip * part, part), part), pl.ds(0, width)
        part = wide // 4
        half = feature // 2
        return pl.ds(pl.multiple_of(chip * part, 16), part), pl.ds(pl.multiple_of(core * half, half), half)

    def full(m):
        return (wo if m % 2 else wq).at[m // 2]

    def half_of(m, s, which):
        half = feature // 2
        spot = pl.ds(pl.multiple_of(which * half, half), half)
        return full(m).at[s, spot, :] if m % 2 else full(m).at[s, :, spot]

    def own(m):
        return (wo_in if m % 2 else wq_in).at[m // 2]

    load = pltpu.make_async_copy(tokens_in, tokens, sem_t)
    load.start()
    locals_ = [pltpu.make_async_copy(own(m), full(m).at[lon], sem_l.at[m]) for m in range(4)]

    def prepare_tokens():
        load.wait()
        edgef[...] = jnp.zeros_like(edgef)
        for j in range(cols):
            line = tokens[j].astype(F32)
            pad[1 + j, 8 : 8 + rows, :] = line
            edgef[0, j : j + 1, :] = line[0:1]
            edgef[1, j : j + 1, :] = line[rows - 1 : rows]
            if j in (0, cols - 1):
                for a, r in ((0, 0), (1, rows - 1)):
                    for b in range(8):
                        corner[a, j // (cols - 1), b : b + 1, :] = line[r : r + 1, 128 * b : 128 * b + 128]
        edge[...] = edgef[...].astype(BF16)

    def prepare_tables():
        def select(shape, index_of):
            to = lax.broadcasted_iota(jnp.int32, (shape[0], 1), 0)
            fro = lax.broadcasted_iota(jnp.int32, shape, 1)
            return jnp.where(fro == index_of(to), 1.0, 0.0).astype(BF16)

        turn[0] = select((count, count), lambda t: jnp.where(
            lax.rem(t, STEP0) < cols, lax.rem(t, STEP0) * STEP1 + t // STEP0, -1))
        turn[1] = select((count, count), lambda t: jnp.where(
            lax.rem(t, STEP1) < rows, lax.rem(t, STEP1) * STEP0 + t // STEP1, -1))
        squeeze[...] = select((PACKED, count), lambda t: jnp.where(
            t < cols * rows, (t // rows) * STEP1 + lax.rem(t, rows), -1))
        expand[0] = select((count, PACKED), lambda t: jnp.where(
            lax.rem(t, STEP0) < cols, lax.rem(t, STEP0) * rows + t // STEP0, -1))
        expand[1] = select((count, PACKED), lambda t: jnp.where(
            lax.rem(t, STEP1) < rows, (t // STEP1) * rows + lax.rem(t, STEP1), -1))

        lane = lax.broadcasted_iota(jnp.int32, bias.shape[1:], 1)
        row = lax.broadcasted_iota(jnp.int32, bias.shape[1:], 0)
        same = lax.rem(lane // STEP0, 2) == lax.rem(row // STEP0, 2)
        bias[0] = jnp.where(same & (lax.rem(lane, STEP0) < cols), 0.0, -jnp.inf)
        bias[1] = jnp.where(lax.rem(lane, STEP1) < rows, 0.0, -jnp.inf)

    prepare_tables()
    pl.semaphore_wait(barrier, len(greet))

    pending = []

    def launch(copy):
        copy.start()
        pending.append(copy)

    def send_z(m, which=(0, 1, 2)):
        at, lanes = piece(m, here)

        def copy(k):
            return remote(
                own(m).at[at, lanes], full(m).at[lon, at, lanes],
                sem_zs.at[m, k], sem_w.at[m, lon, here], (ens, lat, others[k]),
            )

        for k in which:
            if k < 2:
                launch(copy(k))
            else:
                @pl.when(inner)
                def _():
                    copy(2).start()

    def arrived(m, s, chip):
        at, lanes = piece(m, chip)
        spot = full(m).at[s, at, lanes]
        remote(spot, spot, sem_zs.at[m, 0], sem_w.at[m, s, chip], dev_core).wait_recv()

    def pass_on(m, s, chip, send, device):
        at, lanes = piece(m, chip)
        spot = full(m).at[s, at, lanes]
        return remote(spot, spot, send, sem_w.at[m, s, chip], device)

    def z_in(m, i):
        s = others[i]
        arrived(m, s, here)
        launch(pass_on(m, s, here, sem_fs.at[m, i, 0], dev_x))
        launch(pass_on(m, s, here, sem_fs.at[m, i, 1], dev_y))
        if i == 2:
            @pl.when(inner)
            def _():
                pass_on(m, s, here, sem_zs.at[m, 3], (ens, lat, others[1])).start()

    def xy_in(m, i):
        s = others[i]
        arrived(m, s, at_x)
        if (m + i) % 2 == 0:
            launch(pass_on(m, s, at_x, sem_fs.at[m, i, 2], dev_y))
        arrived(m, s, at_y)
        if (m + i) % 2 == 1:
            launch(pass_on(m, s, at_y, sem_fs.at[m, i, 2], dev_x))

    def diag_in(m, i):
        s = others[i]
        arrived(m, s, at_xy)
        launch(remote(half_of(m, s, core), half_of(m, s, core), sem_cs.at[m, i], sem_c.at[m, i], dev_core))

    def whole(m, i):
        spot = half_of(m, others[i], 1 - core)
        remote(spot, spot, sem_cs.at[m, i], sem_c.at[m, i], dev_core).wait_recv()

    halos = [
        (tokens.at[cols - 1], hcol.at[0], (ens, lat, east)),
        (tokens.at[0], hcol.at[1], (ens, lat, west)),
        (edge.at[1], hrow.at[0], (ens, south, lon)),
        (edge.at[0], hrow.at[1], (ens, north, lon)),
        (corner.at[1, 1], hcor.at[0], (ens, south, east)),
        (corner.at[1, 0], hcor.at[1], (ens, south, west)),
        (corner.at[0, 1], hcor.at[2], (ens, north, east)),
        (corner.at[0, 0], hcor.at[3], (ens, north, west)),
    ]
    hcopies = [remote(a, b, sem_hs.at[k], sem_hr.at[k], dev) for k, (a, b, dev) in enumerate(halos)]

    def halo_in():
        for copy in hcopies:
            copy.wait_recv()
        for side, place in ((0, 0), (1, 1 + cols)):
            pad[place, 8 : 8 + rows, :] = hcol[side].astype(F32)
        for k, (spot, inside) in enumerate(((7, lat > 0), (8 + rows, lat < nlat - 1))):
            keep = jnp.where(inside, 1.0, 0.0).astype(F32)
            line = hrow[k].astype(F32) * keep
            for j in range(cols):
                pad[1 + j, spot : spot + 1, :] = line[j : j + 1]
            for b in range(8):
                lanes = slice(128 * b, 128 * b + 128)
                pad[0, spot : spot + 1, lanes] = hcor[2 * k, b : b + 1, :] * keep
                pad[1 + cols, spot : spot + 1, lanes] = hcor[2 * k + 1, b : b + 1, :] * keep

    sent = 24

    def rms(values, k):
        scaled = values * lax.rsqrt(jnp.mean(values * values, axis=-1, keepdims=True) + 1e-06)
        return (scaled * gain[k : k + 1, :]).astype(BF16)

    def conv(low, high):
        taps = conv_w[...].astype(F32)
        bias = conv_b[...].astype(F32).reshape(1, feature)
        alive = lax.broadcasted_iota(jnp.int32, (sent, 1), 0) < rows

        def conv_line(j, carry):
            total = pad[j + 1, 8 : 8 + sent, :] + bias
            for a in range(3):
                for b in range(3):
                    total = total + taps[3 * a + b : 3 * a + b + 1] * pad[j + b, 7 + a : 7 + a + sent, :]
            total = jnp.where(alive, total, 0.0)
            rounded = jnp.concatenate([total, jnp.zeros((STEP1 - sent, feature), F32)], axis=0).astype(BF16)
            spot = pl.ds(pl.multiple_of(j * STEP1, STEP1), STEP1)
            cur[spot, :] = rounded
            normed[spot, :] = rms(rounded.astype(F32), 0)
            return carry

        lax.fori_loop(low, high, conv_line, 0, unroll=True)

    def halves(block):
        left = lax.broadcasted_iota(jnp.int32, block.shape, 1) < HD
        swapped = jnp.concatenate([block[:, HD:], block[:, :HD]], axis=1)
        zero = jnp.zeros_like(block)
        keys = (jnp.where(left, block, zero), jnp.where(left, zero, swapped))
        values = (jnp.where(left, swapped, zero), jnp.where(left, zero, block))
        return keys, values

    def contract(a, b):
        return lax.dot_general(a, b, (((1,), (1,)), ((), ())), preferred_element_type=F32)

    def attend(g, block_of, low, high, which):
        pairs = HEADS // KV // 2
        span = 4 * STEP1
        sides = lax.broadcasted_iota(jnp.int32, (span, 2 * HD), 1) < HD
        ones = [jnp.where(sides, 1.0, 0.0).astype(BF16), jnp.where(sides, 0.0, 1.0).astype(BF16)]
        base = g * pairs

        def spot_of(r):
            return pl.ds(pl.multiple_of(r * STEP1, STEP1), STEP1)

        def score(r, carry):
            spot = spot_of(r)
            kh, vh = halves(block_of(spot))
            query = jnp.concatenate(
                [proj[spot, (base + p) * 128 : (base + p + 1) * 128] for p in range(pairs)], axis=0
            )
            for half in range(2):
                held[r, half] = contract(query, kh[half]) + bias[which]
            return carry

        def soften(r, carry):
            for half in range(2):
                scores = held[r, half]
                expon[r, half] = jnp.exp(scores - jnp.max(scores, axis=-1, keepdims=True)).astype(BF16)
            return carry

        def mix(r, carry):
            spot = spot_of(r)
            kh, vh = halves(block_of(spot))
            both = None
            for half in range(2):
                blend = jnp.concatenate([vh[half], ones[half]], axis=1)
                term = jnp.dot(expon[r, half], blend, preferred_element_type=F32)
                both = term if both is None else both + term
            mixed = (both[:, : 2 * HD] / both[:, 2 * HD :]).astype(BF16)
            for p in range(pairs):
                att[spot, (base + p) * 128 : (base + p + 1) * 128] = mixed[p * STEP1 : (p + 1) * STEP1]
            return carry

        for phase in (score, soften, mix):
            lax.fori_loop(low, high, phase, 0, unroll=True)

    def wide_rows(k, low, high):
        return wq.at[k].reshape(nlon * wide, feature)[low:high, :]

    def query_of(k, source, low, high):
        for t in range(low, high, 256):
            proj[:, t : t + 256] = (contract(source[...], wide_rows(k, t, t + 256)) * HD ** (-0.5)).astype(BF16)

    def keyval_rows(k, g):
        low = feature + g * HD
        return [wide_rows(k, low, low + HD), wide_rows(k, low + KV * HD, low + KV * HD + HD)]

    def send_kv0(g):
        kvs0[g] = jnp.dot(
            squeeze[...], contract(normed[...], jnp.concatenate(keyval_rows(0, g), axis=0)).astype(BF16),
            preferred_element_type=F32,
        ).astype(BF16)

        def copy(k):
            return remote(
                kvs0.at[g], kv0.at[g, lon], sem_ks.at[g, k], sem_kr.at[g, lon], (ens, lat, others[k])
            )

        launch(copy(0))
        launch(copy(1))

        @pl.when(inner)
        def _():
            copy(2).start()

        kv0[g, lon] = kvs0[g]

    def kv0_in(g, i):
        spot = kv0.at[g, others[i]]
        remote(spot, spot, sem_ks.at[g, 0], sem_kr.at[g, others[i]], dev_core).wait_recv()

    def relay_kv0(g):
        kv0_in(g, 2)

        @pl.when(inner)
        def _():
            spot = kv0.at[g, others[2]]
            remote(spot, spot, sem_ks.at[g, 3], sem_kr.at[g, others[2]], (ens, lat, others[1])).start()

    def unfold0(g):
        for s in range(nlon):
            kvt[g, s] = jnp.dot(expand[0], kv0[g, s], preferred_element_type=F32).astype(BF16)

    def send_kv1():
        mixed = contract(normed[...], jnp.concatenate(keyval_rows(1, 0) + keyval_rows(1, 1), axis=0)).astype(BF16)
        kvs1[...] = jnp.dot(squeeze[...], mixed, preferred_element_type=F32).astype(BF16)
        launch(remote(kvs1, kv1.at[lat], sem_js.at[0], sem_jr.at[lat], dev_x))
        launch(remote(kvs1, kv1.at[lat], sem_js.at[1], sem_jr.at[lat], dev_core))
        kvl[lat] = mixed

    def kv1_in(s):
        spot = kv1.at[s]
        remote(spot, spot, sem_js.at[0], sem_jr.at[s], dev_core).wait_recv()

    def share_kv1():
        kv1_in(lat_x)
        launch(remote(kv1.at[lat_x], kv1.at[lat_x], sem_js.at[2], sem_jr.at[lat_x], dev_core))

    def unfold1(s):
        kvl[s] = jnp.dot(expand[1], kv1[s], preferred_element_type=F32).astype(BF16)

    def back(k, values, s):
        lanes = pl.ds(pl.multiple_of(s * width, width), width)
        return (cur[:, lanes].astype(F32) + jnp.dot(values[...], wo[k, s], preferred_element_type=F32)).astype(BF16)

    def gathered(g):
        return lambda spot: jnp.concatenate([kvt[g, s, spot, :] for s in range(nlon)], axis=0)

    def lined(g):
        return lambda spot: jnp.concatenate(
            [kvl[s, spot, g * 128 : g * 128 + 128] for s in range(nlat)], axis=0
        )

    def norm_row(i, carry):
        spot = pl.ds(pl.multiple_of(i * STEP1, STEP1), STEP1)
        normed[spot, :] = rms(cur[spot, :].astype(F32), 1)
        return carry

    def back0():
        for s in range(nlon):
            cur[:, s * width : (s + 1) * width] = back(0, turned, s)

    def back1(s):
        lanes = pl.ds(pl.multiple_of(s * width, width), width)
        out[:, :, lanes] = back(1, att, s).reshape(cols, STEP1, width)[:, :rows, :]

    def attend0(g, low, high):
        attend(g, gathered(g), low, high, 0)

    def attend1(g, low, high):
        attend(g, lined(g), low, high, 1)

    send_z(0, (0, 1, 2))
    prepare_tokens()
    for copy in hcopies:
        copy.start()
    for copy in locals_:
        copy.start()
    z_in(0, 0)
    z_in(0, 1)
    send_z(2, (0, 1, 2))
    z_in(0, 2)
    send_z(1, (0, 1, 2))
    xy_in(0, 1)
    xy_in(0, 0)
    xy_in(0, 2)
    z_in(2, 1)
    diag_in(0, 0)
    z_in(2, 0)
    send_z(3, (0, 1, 2))
    diag_in(0, 2)
    halo_in()
    z_in(1, 1)
    whole(0, 0)
    z_in(2, 2)
    conv(0, 6)
    diag_in(0, 1)
    z_in(1, 0)
    whole(0, 2)
    conv(6, cols)
    z_in(1, 2)
    turned[...] = jnp.dot(turn[0], normed[...], preferred_element_type=F32).astype(BF16)
    xy_in(2, 0)
    whole(0, 1)
    locals_[0].wait()
    send_kv0(0)
    xy_in(2, 1)
    send_kv0(1)
    xy_in(1, 0)
    query_of(0, turned, 0, feature // 2)
    xy_in(1, 2)
    xy_in(1, 1)
    query_of(0, turned, feature // 2, feature)
    xy_in(2, 2)
    z_in(3, 2)
    diag_in(1, 0)
    z_in(3, 0)
    relay_kv0(0)
    diag_in(1, 1)
    kv0_in(0, 0)
    kv0_in(0, 1)
    unfold0(0)
    diag_in(1, 2)
    attend0(0, 0, rows // 2)
    diag_in(2, 0)
    diag_in(2, 1)
    relay_kv0(1)
    kv0_in(1, 0)
    kv0_in(1, 1)
    whole(1, 1)
    unfold0(1)
    diag_in(2, 2)
    z_in(3, 1)
    attend0(1, 0, rows // 2)
    xy_in(3, 0)
    whole(1, 2)
    whole(1, 0)
    turned[...] = jnp.dot(turn[1], att[...], preferred_element_type=F32).astype(BF16)
    whole(2, 0)
    locals_[1].wait()
    back0()
    lax.fori_loop(0, count // STEP1, norm_row, 0, unroll=True)
    whole(2, 2)
    whole(2, 1)
    locals_[2].wait()
    send_kv1()
    xy_in(3, 1)
    xy_in(3, 2)
    query_of(1, normed, 0, feature // 2)
    query_of(1, normed, feature // 2, feature)
    diag_in(3, 1)
    share_kv1()
    unfold1(lat_x)
    kv1_in(lat_core)
    unfold1(lat_core)
    diag_in(3, 0)
    diag_in(3, 2)
    kv1_in(lat_xc)
    unfold1(lat_xc)
    attend1(0, 0, cols)
    attend1(1, 0, cols)
    whole(3, 0)
    locals_[3].wait()
    back1(lon)
    back1(others[0])
    whole(3, 2)
    whole(3, 1)
    back1(others[1])
    back1(others[2])
    for copy in hcopies + pending:
        copy.wait_send()

    @pl.when(inner)
    def _():
        for m in range(4):
            at, lanes = piece(m, here)
            spot = full(m).at[0, at, lanes]
            for k in (2, 3):
                remote(spot, spot, sem_zs.at[m, k], sem_w.at[m, 0, here], dev_core).wait_send()
        for g in range(KV):
            for k in (2, 3):
                remote(kvs0.at[g], kvs0.at[g], sem_ks.at[g, k], sem_kr.at[g, 0], dev_core).wait_send()


def fused(tokens, qkv_weight, out_weight, norm_gain, conv_weight, conv_bias, nlat, nlon):
    tokens, qkv_weight = jnp.swapaxes(tokens, 0, 1), jnp.swapaxes(qkv_weight, 1, 2)
    cols, rows, feature = tokens.shape
    count = rows * STEP0
    vmem = pl.BlockSpec(memory_space=pltpu.VMEM)
    hbm = pl.BlockSpec(memory_space=pl.ANY)
    dma = pltpu.SemaphoreType.DMA
    result = pl.pallas_call(
        step_kernel,
        out_shape=jax.ShapeDtypeStruct(tokens.shape, BF16),
        in_specs=[hbm, hbm, hbm, vmem, vmem, vmem],
        out_specs=vmem,
        scratch_shapes=[
            pltpu.VMEM(tokens.shape, BF16),
            pltpu.VMEM((2, nlon) + qkv_weight.shape[1:], BF16),
            pltpu.VMEM((2, nlon) + out_weight.shape[1:], BF16),
            pltpu.VMEM((cols + 2, 40, feature), F32),
            pltpu.VMEM((2, 16, feature), F32),
            pltpu.VMEM((2, 16, feature), BF16),
            pltpu.VMEM((2, 2, 8, 128), F32),
            pltpu.VMEM((2, rows, feature), BF16),
            pltpu.VMEM((2, 16, feature), BF16),
            pltpu.VMEM((4, 8, 128), F32),
            pltpu.VMEM((count, feature), BF16),
            pltpu.VMEM((count, feature), BF16),
            pltpu.VMEM((count, feature), BF16),
            pltpu.VMEM((2, count, count), BF16),
            pltpu.VMEM((PACKED, count), BF16),
            pltpu.VMEM((2, count, PACKED), BF16),
            pltpu.VMEM((2, HEADS // KV // 2 * STEP1, 4 * STEP1), F32),
            pltpu.VMEM((cols, 2, HEADS // KV // 2 * STEP1, 4 * STEP1), F32),
            pltpu.VMEM((cols, 2, HEADS // KV // 2 * STEP1, 4 * STEP1), BF16),
            pltpu.VMEM((count, feature), BF16),
            pltpu.VMEM((count, feature), BF16),
            pltpu.VMEM((KV, PACKED, 2 * HD), BF16),
            pltpu.VMEM((KV, nlon, PACKED, 2 * HD), BF16),
            pltpu.VMEM((KV, nlon, count, 2 * HD), BF16),
            pltpu.VMEM((PACKED, KV * 2 * HD), BF16),
            pltpu.VMEM((nlat, PACKED, KV * 2 * HD), BF16),
            pltpu.VMEM((nlat, count, KV * 2 * HD), BF16),
            dma,
            dma((4,)),
            dma((4, 4)),
            dma((4, nlon, 4)),
            dma((4, 3, 3)),
            dma((4, 3)),
            dma((4, 3)),
            dma((8,)),
            dma((8,)),
            dma((KV, 4)),
            dma((KV, nlon)),
            dma((3,)),
            dma((nlat,)),
        ],
        compiler_params=pltpu.CompilerParams(
            collective_id=0, has_side_effects=True, vmem_limit_bytes=56 * 2**20
        ),
    )(tokens, qkv_weight, out_weight, norm_gain, conv_weight, conv_bias)
    return jnp.swapaxes(result, 0, 1)


def entry(tokens, qkv_weight, out_weight, norm_gain, conv_weight, conv_bias):
    nens, nlat, nlon = (lax.axis_size(name) for name in ("ens", "lat", "lon"))
    if (nens, nlat, nlon) == (2, 4, 4) and tokens.shape[:2] == (22, 11):
        return fused(
            tokens, qkv_weight, out_weight, norm_gain, conv_weight, conv_bias, nlat, nlon
        )
    return shards(tokens, qkv_weight, out_weight, norm_gain, conv_weight, conv_bias)


def solution(mesh):
    in_specs = (
        P(("ens", "lat"), "lon", None),
        P(None, None, "lon"),
        P(None, None, "lon"),
        P(),
        P(),
        P(),
    )
    out_specs = P(("ens", "lat"), "lon", None)
    return jax.shard_map(entry, mesh=mesh, in_specs=in_specs, out_specs=out_specs, check_vma=False)
```
